256 devices in a mesh: seq: 32 (over y, z), chan: 8 (over x, core).
Axes of the slice: x: 4, y: 4, z: 8, core: 2. Of those that a mesh axis runs over, the one named last changes fastest.
Arguments:
- features: bfloat16 [3, 8192, 8192], P(None, 'seq', 'chan'), may hold values from -6 to 6
- short_filter: bfloat16 [7, 3, 512], P(None, None, 'chan'), may hold values from -3 to 3
- decay: float32 [16, 8192], P(None, 'chan'), may hold values from 2.4414063e-05 to 0.05
- angle_rate: float32 [16, 8192], P(None, 'chan'), may hold values from -1 to 1
- residues: float32 [2, 16, 8192], P(None, None, 'chan'), may hold values from -0.12 to 0.12
- skip: float32 [8192], P('chan'), may hold values from -4 to 4
- entry_states: float32 [8, 2, 16, 8192], P(None, None, None, 'chan'), may hold values from -48 to 48
- segment_ids: int32 [8192], replicated, may hold values from 0 to 7, never falling along the last dimension, each value on 1 to 2048 neighbouring positions
- state_ids: int32 [8], replicated, may hold values from 0 to 7
- out_weight: bfloat16 [8192, 8192], P('chan', 'seq'), may hold values from -0.125 to 0.125
Outputs:
- mixed_out: bfloat16 [8192, 8192], P('seq', 'chan')
The draws below stay inside these ranges and needn't reach their ends.
Inputs may be any that keep to these rules, and one draw needn't show every extreme that they name: `segment_ids`: never falls along the window; each of the 8 records holds 1 to 2048 positions and one holds exactly 2048.
All inputs are finite; a program needn't handle non-finite values.
Results may differ from the reference program's by a relative error of at most 0.025.
Values may be sent and summed in bfloat16 or wider, within the bound.
No kernel may reach another device: no remote copies, remote signals or barrier semaphores. Data moves between devices by JAX's collectives and lax.ppermute only.
A program may use at most 128 MiB of HBM per device.

```python
import math
import jax
import jax.numpy as jnp
import numpy as np
from jax import lax

D = 8192
MODES = 16
SHORT = 7
NREC = 8
NSTATE = 8
GROUPS = 512
TOKENS = 8192
RECORD_MOST = 2048
N_CHAN = 8


def touch_ends(values, stream_key, least, top_value):
    place = [jax.random.randint(jax.random.fold_in(stream_key, axis), (), 0, length) for axis, length in enumerate(values.shape)]
    main_axis = values.shape.index(max(values.shape))
    beside = place[:main_axis] + [(place[main_axis] + 1) % values.shape[main_axis]] + place[main_axis + 1:]
    return values.at[tuple(place)].set(least).at[tuple(beside)].set(top_value)


def strengthened(values, own_key, source, target, parts, factor):
    owner, partner = [(jnp.arange(values.shape[position]) // (values.shape[position] // parts)).reshape([-1 if axis == position else 1 for axis in range(values.ndim)]) for position in (source, target)]
    chosen = jax.random.permutation(own_key, parts)[partner]
    strong = (owner == chosen) | (owner == (partner + parts // 2) % parts)
    return jnp.where(strong, factor * values, values)


def shard_levels(key, dims, split, least, largest):
    def one(dim, shards_of):
        steps = jax.random.uniform(jax.random.fold_in(jax.random.fold_in(key, 6), dim), (shards_of,), jnp.float32, least / len(split), largest / len(split))
        return jnp.repeat(jnp.exp(steps), dims[dim] // shards_of).reshape((-1,) + (1,) * (len(dims) - dim - 1))

    loudness = one(*split[0])
    for cut in split[1:]:
        loudness = loudness * one(*cut)
    return loudness


def profile(amount, total, reach, skew):
    portions = [(1 << 20) // math.isqrt(standing ** skew) + 1 for standing in range(2, amount + 1)]
    surplus, given = total - reach - (amount - 1), [1] * (amount - 1)
    while surplus > 0:
        candidates = [i for i in range(amount - 1) if given[i] < reach]
        pool, remaining = sum([portions[i] for i in candidates]), surplus
        for i in candidates:
            more = min(reach - given[i], max(1, remaining * portions[i] // pool), surplus)
            given[i] = given[i] + more
            surplus = surplus - more
    return np.array([reach] + given)


def uneven_parts(rng, count, total, bound, skew):
    if count == 2:
        one = jax.random.randint(rng, (), max(1, total - bound), min(bound, total - 1) + 1)
        return jnp.stack([one, total - one])
    lengths = jnp.asarray(profile(count, total, bound, skew), jnp.int32)
    twos = (count - 1) // 2
    giver, receiver = lengths[1:1 + 2 * twos:2], lengths[2:2 + 2 * twos:2]
    slack = jnp.minimum(giver - 1, bound - receiver)
    moved = jax.random.randint(jax.random.fold_in(rng, 1), (twos,), 0, 1 << 20) % (slack + 1)
    lengths = lengths.at[1:1 + 2 * twos:2].set(giver - moved).at[2:2 + 2 * twos:2].set(receiver + moved)
    return lengths[jax.random.permutation(jax.random.fold_in(rng, 2), count)]


def bell_draw(rng, dims, spread, limit, cuts=(), held_as=jnp.bfloat16):
    gain = shard_levels(rng, dims, cuts, -0.22, 0.18) if cuts else 1.0
    result = jax.random.normal(rng, dims, jnp.float32) * spread * gain
    return jnp.minimum(jnp.maximum(result, -limit), limit).astype(held_as)


def bell_draw_with(own_key, shape, scale, reach, cuts, heavy, dtype=jnp.bfloat16):
    drawn = scale * jax.random.normal(own_key, shape, jnp.float32)
    if cuts:
        drawn = drawn * shard_levels(own_key, shape, cuts, -0.22, 0.18)
    return jnp.clip(strengthened(drawn, jax.random.fold_in(own_key, 3), *heavy), -reach, reach).astype(dtype)


def setup_inputs(seed: int = 0) -> dict:
    streams_of = jax.random.split(jax.random.key(seed), 11)
    features = bell_draw(streams_of[0], (3, TOKENS, D), 1.0, 6.0, ((1, 32), (2, 8)))
    short_filter = bell_draw(streams_of[1], (SHORT, 3, GROUPS), 0.45, 3.0, ((2, 8),))
    decay = jnp.clip(jnp.exp(math.log(0.05) - 7.624619 * jax.random.uniform(streams_of[2], (MODES, D), jnp.float32) ** shard_levels(streams_of[2], (MODES, D), ((1, 8),), -0.2, 0.2)), 2.441406286379788e-05, 0.05)
    angle_rate = jnp.clip(jax.random.uniform(streams_of[3], (MODES, D), jnp.float32, -1.0, 1.0) * shard_levels(streams_of[3], (MODES, D), ((1, 8),), -0.4, 0.0), -1.0, 1.0)
    residues = bell_draw(streams_of[4], (2, MODES, D), 0.02, 0.12, ((2, 8),), jnp.float32)
    skip = bell_draw(streams_of[5], (D,), 1.0, 4.0, ((0, 8),), jnp.float32)
    entry_states = bell_draw(streams_of[6], (NSTATE, 2, MODES, D), 8.0, 48.0, ((3, 8),), jnp.float32)
    segment_ids = jnp.searchsorted(jnp.cumsum(uneven_parts(streams_of[7], NREC, TOKENS, RECORD_MOST, 1)), jnp.arange(TOKENS), side="right").astype(jnp.int32)
    state_ids = touch_ends(jax.random.randint(streams_of[8], (NREC,), 0, NSTATE), jax.random.fold_in(streams_of[8], 1), 0, NSTATE - 1).astype(jnp.int32)
    out_weight = bell_draw_with(streams_of[9], (D, D), D ** -0.5, 0.125, ((0, 8), (1, 32)), (0, 1, 32, 2.75))
    return {"features": features, "short_filter": short_filter, "decay": decay, "angle_rate": angle_rate, "residues": residues, "skip": skip, "entry_states": entry_states, "segment_ids": segment_ids, "state_ids": state_ids, "out_weight": out_weight}


def move_channels(array, axis, blocks, block):
    shape = array.shape
    reshaped = array.reshape(shape[:axis] + (blocks, block) + shape[axis + 1:])
    return jnp.moveaxis(reshaped, axis, 0)


def reference(features, short_filter, decay, angle_rate, residues, skip, entry_states, segment_ids, state_ids, out_weight):
    length = features.shape[1]
    width = features.shape[2]
    taps = short_filter.shape[0]
    group_size = width // short_filter.shape[2]
    block = math.gcd(width, 1024)
    blocks = width // block
    starts = jnp.concatenate([jnp.ones((1,), jnp.bool_), segment_ids[1:] != segment_ids[:-1]])
    entry_index = state_ids[segment_ids].astype(jnp.int32)
    short_all = jnp.repeat(short_filter.astype(jnp.float32), group_size, axis=2)
    inputs = (move_channels(features, 2, blocks, block), move_channels(short_all, 2, blocks, block),
              move_channels(decay, 1, blocks, block),
              move_channels(angle_rate, 1, blocks, block), move_channels(residues, 2, blocks, block),
              move_channels(skip, 0, blocks, block), move_channels(entry_states, 3, blocks, block))

    def channel_block(packed):
        streams, short_part, decay_part, angle_part, residue_part, skip_part, entry_part = packed
        values = streams.astype(jnp.float32)
        featured = jnp.zeros(values.shape, jnp.float32)
        for offset in range(taps):
            shifted = jnp.pad(values, ((0, 0), (offset, 0), (0, 0)))[:, :length]
            shifted_ids = jnp.pad(segment_ids, (offset, 0), constant_values=-1)[:length]
            same = (shifted_ids == segment_ids).astype(jnp.float32)
            featured = featured + short_part[offset][:, None, :] * shifted * same[None, :, None]
        product = lax.optimization_barrier((featured[1] * featured[2]).astype(jnp.bfloat16))
        product_f = product.astype(jnp.float32)
        magnitude = jnp.exp(-decay_part)
        pole_re = magnitude * jnp.cos(angle_part)
        pole_im = magnitude * jnp.sin(angle_part)

        def modal_step(state, inputs_now):
            state_re, state_im = state
            value, flag, pick = inputs_now
            entering = lax.dynamic_index_in_dim(entry_part, pick, 0, keepdims=False)
            before_re = jnp.where(flag, entering[0], state_re)
            before_im = jnp.where(flag, entering[1], state_im)
            new_re = pole_re * before_re - pole_im * before_im + value[None, :]
            new_im = pole_re * before_im + pole_im * before_re
            output = jnp.sum(residue_part[0] * new_re - residue_part[1] * new_im, axis=0)
            return (new_re, new_im), output

        zeros = jnp.zeros(pole_re.shape, jnp.float32)
        unused, modal = lax.scan(modal_step, (zeros, zeros), (product_f, starts, entry_index))
        return (featured[0] * (modal + skip_part[None, :] * product_f)).astype(jnp.bfloat16)

    gated_blocks = lax.map(channel_block, inputs)
    gated = jnp.moveaxis(gated_blocks, 0, 1).reshape(length, width)
    shard = width // N_CHAN
    total = jnp.zeros((length, width), jnp.float32)
    for index in range(N_CHAN):
        part = jnp.dot(gated[:, index * shard:(index + 1) * shard], out_weight[index * shard:(index + 1) * shard],
                       preferred_element_type=jnp.float32)
        total = total + lax.optimization_barrier(part.astype(jnp.bfloat16)).astype(jnp.float32)
    return total.astype(jnp.bfloat16)
```

```python
import functools

import jax
import jax.numpy as jnp
from jax import lax
from jax.experimental import pallas as pl
from jax.experimental.pallas import tpu as pltpu
from jax.sharding import Mesh
from jax.sharding import PartitionSpec as P

F32 = jnp.float32
BF16 = jnp.bfloat16
ROWS = 256
CH = 1024
LANES = 128
TILES = CH // LANES
MODES = 16
TAPS = 7
GAP = 9
BLOCK = GAP * TILES
VMEM_LIMIT = 56 * 1024 * 1024


def spread(scratch, base, value):
    for j in range(TILES):
        scratch[pl.ds(base + j * GAP, 8), :] = value[:, j * LANES : (j + 1) * LANES]


def row(scratch, base, r):
    return scratch[pl.ds(base + r, TILES, stride=GAP), :]


def record_of(ids, position):
    return jnp.where(position < 0, -1, ids[jnp.maximum(position, 0)])


def scan_kernel(
    dev_ref, ids, picks, feat, border, filt, decay, angle, res, skip, entry,
    final_out, pole_out, power_out, query_out, base_out,
    streams, tables, product, states, small,
):
    position = dev_ref[0] * ROWS
    for half in range(2):
        rows = slice(8 * half, 8 * half + 8)
        mag = jnp.exp(-decay[rows, :])
        ang = angle[rows, :]
        parts = (mag * jnp.cos(ang), mag * jnp.sin(ang), res[0, rows, :], res[1, rows, :])
        for n, part in enumerate(parts):
            spread(small, n * BLOCK, part)
        for n in range(4):
            for r in range(8):
                tables[n, 8 * half + r] = row(small, n * BLOCK, r)
    for m in range(MODES):
        pole_out[0, m] = tables[0, m]
        pole_out[1, m] = tables[1, m]
        re, im = tables[0, m], tables[1, m]
        for _ in range(8):
            re, im = re * re - im * im, 2.0 * re * im
        power_out[0, m] = re
        power_out[1, m] = im
    spread(small, 0, jnp.broadcast_to(skip[...], (8, CH)))
    skip_row = row(small, 0, 0)

    for i in range(3):
        spread(streams.at[i], 0, border[i].astype(F32))

    def relayout(b, carry):
        for i in range(3):
            value = feat[i, pl.ds(pl.multiple_of(b * 16, 16), 16), :].astype(F32)
            spread(streams.at[i], (2 * b + 1) * BLOCK, value[:8])
            spread(streams.at[i], (2 * b + 2) * BLOCK, value[8:])
        return carry

    lax.fori_loop(0, ROWS // 16, relayout, 0)

    def featurize(b, carry):
        first = position + 8 * b
        plain = record_of(ids, first - 6) == ids[first + 7]

        def outputs(results):
            for t in range(8):
                query_out[8 * b + t] = results[0][t]
                product[8 * b + t] = (results[1][t] * results[2][t]).astype(BF16).astype(F32)

        def rows_of(i):
            return [row(streams.at[i], b * BLOCK, 2 + r) for r in range(6)] + [
                row(streams.at[i], (b + 1) * BLOCK, r) for r in range(8)
            ]

        @pl.when(plain)
        def _():
            results = []
            for i in range(3):
                values = rows_of(i)
                taps = [filt[j, i] for j in range(TAPS)]
                results.append(
                    [sum(taps[j] * values[6 + t - j] for j in range(TAPS)) for t in range(8)]
                )
            outputs(results)

        @pl.when(jnp.logical_not(plain))
        def _():
            same = [
                [
                    (record_of(ids, first + t - j) == ids[first + t]).astype(F32)
                    for j in range(TAPS)
                ]
                for t in range(8)
            ]
            results = []
            for i in range(3):
                values = rows_of(i)
                taps = [filt[j, i] for j in range(TAPS)]
                results.append(
                    [
                        sum(
                            taps[j] * jnp.where(same[t][j] > 0.5, values[6 + t - j], 0.0)
                            for j in range(TAPS)
                        )
                        for t in range(8)
                    ]
                )
            outputs(results)

        return carry

    lax.fori_loop(0, ROWS // 8, featurize, 0)

    for group in range(2):
        modes = range(8 * group, 8 * group + 8)
        for m in range(8):
            states[0, m] = jnp.zeros((8, LANES), F32)
            states[1, m] = jnp.zeros((8, LANES), F32)

        def step(value, re, im, group=group, modes=modes):
            out = None
            for m in range(8):
                pr, pi = tables[0, modes[m]], tables[1, modes[m]]
                new_re = pr * re[m] - pi * im[m] + value
                new_im = pr * im[m] + pi * re[m]
                re[m], im[m] = new_re, new_im
                term = tables[2, modes[m]] * new_re - tables[3, modes[m]] * new_im
                out = term if out is None else out + term
            return out

        def emit(t, value, out, group=group):
            if group == 0:
                base_out[t] = skip_row * value + out
            else:
                base_out[t] = base_out[t] + out

        def block(b, carry, group=group, step=step, emit=emit):
            first = position + 8 * b
            plain = record_of(ids, first - 1) == ids[first + 7]

            @pl.when(plain)
            def _():
                re = [states[0, m] for m in range(8)]
                im = [states[1, m] for m in range(8)]
                for t in range(8):
                    value = product[8 * b + t]
                    emit(8 * b + t, value, step(value, re, im))
                for m in range(8):
                    states[0, m] = re[m]
                    states[1, m] = im[m]

            @pl.when(jnp.logical_not(plain))
            def _():
                def one(t, carry):
                    here = first + t

                    @pl.when(record_of(ids, here - 1) != ids[here])
                    def _():
                        pick = picks[ids[here]]
                        for part in range(2):
                            spread(small, 0, entry[pick, part, 8 * group : 8 * group + 8, :])
                            for m in range(8):
                                states[part, m] = row(small, 0, m)

                    re = [states[0, m] for m in range(8)]
                    im = [states[1, m] for m in range(8)]
                    value = product[8 * b + t]
                    emit(8 * b + t, value, step(value, re, im))
                    for m in range(8):
                        states[0, m] = re[m]
                        states[1, m] = im[m]
                    return carry

                lax.fori_loop(0, 8, one, 0)

            return carry

        lax.fori_loop(0, ROWS // 8, block, 0)
        for part in range(2):
            for m in range(0, 8, 2):
                pair = jnp.concatenate([states[part, m], states[part, m + 1]], axis=0)
                at = 64 * group + 8 * m
                final_out[part, at : at + 16, :] = pair.astype(BF16)


def scan(dev, ids, picks, feat, border, filt, decay, angle, res, skip, entry, interpret=False):
    smem = pl.BlockSpec(memory_space=pltpu.SMEM)
    vmem = pl.BlockSpec(memory_space=pltpu.VMEM)
    wide = (8, LANES)
    return pl.pallas_call(
        scan_kernel,
        out_shape=(
            jax.ShapeDtypeStruct((2, MODES * 8, LANES), BF16),
            jax.ShapeDtypeStruct((2, MODES) + wide, F32),
            jax.ShapeDtypeStruct((2, MODES) + wide, F32),
            jax.ShapeDtypeStruct((ROWS,) + wide, F32),
            jax.ShapeDtypeStruct((ROWS,) + wide, F32),
        ),
        in_specs=[smem, smem, smem] + [vmem] * 8,
        out_specs=(vmem,) * 5,
        scratch_shapes=[
            pltpu.VMEM((3, (ROWS // 8 + 1) * BLOCK, LANES), F32),
            pltpu.VMEM((4, MODES) + wide, F32),
            pltpu.VMEM((ROWS,) + wide, F32),
            pltpu.VMEM((2, 8) + wide, F32),
            pltpu.VMEM((4 * BLOCK, LANES), F32),
        ],
        compiler_params=pltpu.CompilerParams(vmem_limit_bytes=VMEM_LIMIT),
        name="modal_scan",
        interpret=interpret,
    )(dev, ids, picks, feat, border, filt, decay, angle, res, skip, entry)


def carry_kernel(dev_ref, ids, carry, pole, res, query, base, gated_out, tables, added, stage, small):
    position = dev_ref[0] * ROWS
    before = record_of(ids, position - 1)
    for part in range(2):
        for half in range(2):
            spread(small, 0, res[part, 8 * half : 8 * half + 8, :])
            for r in range(8):
                tables[part, 8 * half + r] = row(small, 0, r)
    for m in range(MODES):
        cr, ci = carry[0, m], carry[1, m]
        rr, ri = tables[0, m], tables[1, m]
        tables[0, m] = rr * cr - ri * ci
        tables[1, m] = rr * ci + ri * cr

    for group in range(2):
        modes = range(8 * group, 8 * group + 8)

        def block(b, carry, modes=modes, group=group):
            first = position + 8 * b

            @pl.when(ids[first] == before)
            def _():
                re = [tables[0, m] for m in modes]
                im = [tables[1, m] for m in modes]
                for t in range(8):
                    out = None
                    for m in range(8):
                        pr, pi = pole[0, modes[m]], pole[1, modes[m]]
                        re[m], im[m] = pr * re[m] - pi * im[m], pr * im[m] + pi * re[m]
                        out = re[m] if out is None else out + re[m]
                    out = jnp.where(ids[first + t] == before, out, 0.0)
                    if group == 0:
                        added[8 * b + t] = out
                    else:
                        added[8 * b + t] = added[8 * b + t] + out
                for m in range(8):
                    tables[0, modes[m]] = re[m]
                    tables[1, modes[m]] = im[m]

            if group == 0:

                @pl.when(ids[first] != before)
                def _():
                    for t in range(8):
                        added[8 * b + t] = jnp.zeros((8, LANES), F32)

            return carry

        lax.fori_loop(0, ROWS // 8, block, 0)

    def gate(b, carry):
        for half in range(2):
            for t in range(8):
                at = 16 * b + 8 * half + t
                value = query[at] * (base[at] + added[at])
                stage[pl.ds((2 * b + half) * BLOCK + t, TILES, stride=GAP), :] = value
        for j in range(TILES):
            low = stage[pl.ds(2 * b * BLOCK + j * GAP, 8), :]
            high = stage[pl.ds((2 * b + 1) * BLOCK + j * GAP, 8), :]
            both = jnp.concatenate([low, high], axis=0).astype(BF16)
            gated_out[pl.ds(pl.multiple_of(16 * b, 16), 16), j * LANES : (j + 1) * LANES] = both
        return carry

    lax.fori_loop(0, ROWS // 16, gate, 0)


def carried(dev, ids, carry, pole, res, query, base, interpret=False):
    smem = pl.BlockSpec(memory_space=pltpu.SMEM)
    vmem = pl.BlockSpec(memory_space=pltpu.VMEM)
    wide = (8, LANES)
    return pl.pallas_call(
        carry_kernel,
        out_shape=jax.ShapeDtypeStruct((ROWS, CH), BF16),
        in_specs=[smem, smem] + [vmem] * 5,
        out_specs=vmem,
        scratch_shapes=[
            pltpu.VMEM((2, MODES) + wide, F32),
            pltpu.VMEM((ROWS,) + wide, F32),
            pltpu.VMEM((ROWS // 8 * BLOCK, LANES), F32),
            pltpu.VMEM((BLOCK, LANES), F32),
        ],
        compiler_params=pltpu.CompilerParams(vmem_limit_bytes=VMEM_LIMIT),
        name="carry_gate",
        interpret=interpret,
    )(dev, ids, carry, pole, res, query, base)


def product_kernel(core_ref, rows_ref, weight_ref, out_ref):
    out_ref[...] = jnp.dot(rows_ref[...], weight_ref[0], preferred_element_type=F32).astype(BF16)


def partial_products(core, rows, weight):
    return pl.pallas_call(
        product_kernel,
        out_shape=jax.ShapeDtypeStruct((2, 4 * ROWS, CH), BF16),
        grid_spec=pltpu.PrefetchScalarGridSpec(
            num_scalar_prefetch=1,
            grid=(8,),
            in_specs=[
                pl.BlockSpec((4 * ROWS, CH), lambda n, core: (0, 0)),
                pl.BlockSpec((1, CH, 256), lambda n, core: ((n + 4 * core[0]) % 8, 0, 0)),
            ],
            out_specs=pl.BlockSpec((None, 4 * ROWS, 256), lambda n, core: (n // 4, 0, n % 4)),
        ),
        compiler_params=pltpu.CompilerParams(vmem_limit_bytes=VMEM_LIMIT),
        name="partial_products",
    )(core, rows, weight)


def add_complex(own, other, power, keep):
    other = other.astype(F32)
    power = power * keep
    re = power[0] * other[0] - power[1] * other[1]
    im = power[0] * other[1] + power[1] * other[0]
    return own.astype(F32) + jnp.stack([re, im])


def square(power):
    return jnp.stack([power[0] * power[0] - power[1] * power[1], 2.0 * power[0] * power[1]])


def shift_records(value, steps):
    return lax.ppermute(value, ("y", "z"), [(i, i + steps) for i in range(32 - steps)])


def shards(
    features, short_filter, decay, angle_rate, residues, skip, entry_states, segment_ids, state_ids, out_weight
):
    y, z = lax.axis_index("y"), lax.axis_index("z")
    x, core = lax.axis_index("x"), lax.axis_index("core")
    device = y * 8 + z
    weight = lax.all_gather(out_weight, "z", axis=0)
    border = shift_records(features[:, ROWS - 8 :, :], 1)
    filt = jnp.repeat(short_filter.astype(F32), 16, axis=2).reshape(TAPS, 3, 8, LANES)
    dev = device.reshape(1).astype(jnp.int32)
    final, pole, power, query, base = scan(
        dev, segment_ids, state_ids, features, border, filt, decay, angle_rate, residues,
        skip.reshape(1, CH), entry_states,
    )
    power1 = power.reshape(2, MODES * 8, LANES)
    power2 = square(power1)
    power4 = square(power2)

    def keep(count):
        first = (device - count) * ROWS - 1
        last = device * ROWS - 1
        same = segment_ids[jnp.maximum(first, 0)] == segment_ids[jnp.maximum(last, 0)]
        return jnp.logical_and(first >= 0, same).astype(F32)

    e1 = shift_records(final, 1)
    e2 = add_complex(e1, shift_records(e1, 1), power1, keep(1))
    e4 = add_complex(e2, shift_records(e2.astype(BF16), 2), power2, keep(2))
    e8 = add_complex(e4, shift_records(e4.astype(BF16), 4), power4, keep(4))
    gated = carried(dev, segment_ids, e8.reshape(2, MODES, 8, LANES), pole, residues, query, base)

    def offset(owner, y):
        return owner

    rows = [
        lax.ppermute(
            gated,
            ("y", "x"),
            [
                (((b + offset((a + k) % 4, b)) % 4) * 4 + a, b * 4 + a)
                for b in range(4)
                for a in range(4)
            ],
        )
        for k in range(4)
    ]
    rows = jnp.concatenate(rows, axis=0)
    parts = partial_products(core.reshape(1).astype(jnp.int32), rows, weight)
    other = lax.ppermute(parts[1], "core", [(0, 1), (1, 0)])
    pair = (parts[0].astype(F32) + other.astype(F32)).astype(BF16).reshape(4, ROWS, CH)
    total = pair[0].astype(F32)
    for k in range(1, 4):
        total = total + lax.ppermute(pair[k], "x", [(a, (a + k) % 4) for a in range(4)]).astype(F32)
    moves = [
        (b * 4 + a, ((b + offset(a, b)) % 4) * 4 + b) for b in range(4) for a in range(4)
    ]
    return lax.ppermute(total.astype(BF16), ("y", "x"), moves)


def solution(mesh):
    fine = Mesh(mesh.devices.reshape(4, 8, 4, 2), ("y", "z", "x", "core"))
    seq, chan = ("y", "z"), ("x", "core")
    in_specs = (
        P(None, seq, chan),
        P(None, None, chan),
        P(None, chan),
        P(None, chan),
        P(None, None, chan),
        P(chan),
        P(None, None, None, chan),
        P(),
        P(),
        P(chan, seq),
    )
    return jax.shard_map(shards, mesh=fine, in_specs=in_specs, out_specs=P(seq, chan), check_vma=False)
```

```python
import jax
import jax.numpy as jnp
from jax import lax
from jax.experimental import pallas as pl
from jax.experimental.pallas import tpu as pltpu
from jax.sharding import Mesh
from jax.sharding import PartitionSpec as P

F32 = jnp.float32
BF16 = jnp.bfloat16
ROWS = 256
CH = 1024
LANES = 128
TILES = CH // LANES
MODES = 16
TAPS = 7
GROUP = 16
GAP = 9
BLOCK = GAP * TILES
COLS = 256
WIDE = (8, LANES)
MIB = 1024 * 1024
SMEM_SPEC = pl.BlockSpec(memory_space=pltpu.SMEM)
VMEM_SPEC = pl.BlockSpec(memory_space=pltpu.VMEM)


def call(kernel, outs, in_specs, scratch, limit, name, cycles, interpret=False):
    return pl.pallas_call(
        kernel,
        out_shape=outs,
        in_specs=in_specs,
        out_specs=jax.tree.map(lambda out: VMEM_SPEC, outs),
        scratch_shapes=scratch,
        compiler_params=pltpu.CompilerParams(vmem_limit_bytes=limit * MIB),
        cost_estimate=pl.CostEstimate(flops=cycles, transcendentals=0, bytes_accessed=MIB),
        name=name,
        interpret=interpret,
    )


def first_position():
    device = (lax.axis_index("y") * 4 + lax.axis_index("zh")) * 2 + lax.axis_index("zl")
    return device * ROWS


def spread(scratch, base, value):
    for j in range(TILES):
        scratch[pl.ds(base + j * GAP, value.shape[0]), :] = value[:, j * LANES : (j + 1) * LANES]


def row(scratch, base, r):
    return scratch[pl.ds(base + r, TILES, stride=GAP), :]


def record_of(ids, position):
    return jnp.where(position < 0, -1, ids[jnp.maximum(position, 0)])


def prepare_kernel(ids, feat, filt, decay, angle, pole_out, power_out, taps_out, streams_out, edge_out, small):
    position = first_position()
    edge_out[...] = feat[:, ROWS - 8 :, :]
    for half in range(2):
        rows = slice(8 * half, 8 * half + 8)
        mag = jnp.exp(-decay[rows, :])
        ang = angle[rows, :]
        spread(small, 0, mag * jnp.cos(ang))
        spread(small, BLOCK, mag * jnp.sin(ang))
        for r in range(8):
            pole_out[0, 8 * half + r] = row(small, 0, r)
            pole_out[1, 8 * half + r] = row(small, BLOCK, r)
    last = record_of(ids, position - 1)
    keeps = []
    for count in (1, 2, 4, 6):
        before = position - count * ROWS - 1
        keeps.append(jnp.where((before >= 0) & (record_of(ids, before) == last), 1.0, 0.0))
    for m in range(MODES):
        re, im = pole_out[0, m], pole_out[1, m]
        for doubling in range(8):
            re, im = re * re - im * im, 2.0 * re * im
        powers = [(re, im)]
        for doubling in range(2):
            re, im = re * re - im * im, 2.0 * re * im
            powers.append((re, im))
        two = powers[1]
        powers.append((re * two[0] - im * two[1], re * two[1] + im * two[0]))
        for n in range(4):
            power_out[n, 0, m] = powers[n][0] * keeps[n]
            power_out[n, 1, m] = powers[n][1] * keeps[n]
    groups = CH // GROUP
    group = lax.broadcasted_iota(jnp.int32, (groups, CH), 0)
    channel = lax.broadcasted_iota(jnp.int32, (groups, CH), 1)
    widen = jnp.where(channel // GROUP == group, 1.0, 0.0).astype(BF16)
    for i in range(3):
        spread(small, 0, jnp.dot(filt[i], widen, preferred_element_type=F32))
        for j in range(TAPS):
            taps_out[j, i] = row(small, 0, j)

    def lay_out(b, carry):
        for i in range(3):
            value = feat[i, pl.ds(pl.multiple_of(b * 16, 16), 16), :].astype(F32)
            spread(streams_out.at[i], 2 * b * BLOCK, value[:8])
            spread(streams_out.at[i], (2 * b + 1) * BLOCK, value[8:])
        return carry

    lax.fori_loop(0, ROWS // 16, lay_out, 0)


def prepare(ids, feat, filt, decay, angle):
    return call(
        prepare_kernel,
        (
            jax.ShapeDtypeStruct((2, MODES) + WIDE, F32),
            jax.ShapeDtypeStruct((4, 2, MODES) + WIDE, F32),
            jax.ShapeDtypeStruct((TAPS, 3) + WIDE, F32),
            jax.ShapeDtypeStruct((3, ROWS // 8 * BLOCK, LANES), F32),
            jax.ShapeDtypeStruct((3, 8, CH), BF16),
        ),
        [SMEM_SPEC] + [VMEM_SPEC] * 4,
        [pltpu.VMEM((2 * BLOCK, LANES), F32)],
        16,
        "prepare",
        3_000_000,
    )(ids, feat, filt, decay, angle)


def featurized(i, b, before, stream, taps_ref, same):
    values = [row(before[0], before[1], 2 + r) for r in range(6)]
    values += [row(stream, b * BLOCK, r) for r in range(8)]
    taps = [taps_ref[j, i] for j in range(TAPS)]
    outs = []
    for t in range(8):
        out = taps[0] * values[6 + t]
        for j in range(1, TAPS):
            value = values[6 + t - j]
            if same is not None:
                value = jnp.where(same[t][j], value, 0.0)
            out = out + taps[j] * value
        outs.append(out)
    return outs


def featurize(position, ids, which, streams, edge, taps, emit):
    def block(b, before):
        first = position + 8 * b
        plain = record_of(ids, first - 6) == ids[first + 7]

        def run(same):
            emit(b, [featurized(i, b, before(i), streams.at[i], taps, same) for i in which])

        @pl.when(plain)
        def _():
            run(None)

        @pl.when(jnp.logical_not(plain))
        def _():
            run([[record_of(ids, first + t - j) == ids[first + t] for j in range(TAPS)] for t in range(8)])

    block(0, lambda i: (edge, i * BLOCK))

    def step(b, carry):
        block(b, lambda i: (streams.at[i], (b - 1) * BLOCK))
        return carry

    lax.fori_loop(1, ROWS // 8, step, 0)


def run_modes(position, ids, picks, entry, states, small, product, group, step, emit, carry_in=None):
    for part in range(2):
        for m in range(8):
            states[part, m] = jnp.zeros(WIDE, F32) if carry_in is None else carry_in[part, 8 * group + m]

    def block(b, carry):
        first = position + 8 * b
        plain = record_of(ids, first - 1) == ids[first + 7]

        @pl.when(plain)
        def _():
            re = [states[0, m] for m in range(8)]
            im = [states[1, m] for m in range(8)]
            for t in range(8):
                value = product[8 * b + t]
                emit(8 * b + t, value, step(value, re, im))
            for m in range(8):
                states[0, m] = re[m]
                states[1, m] = im[m]

        @pl.when(jnp.logical_not(plain))
        def _():
            def one(t, carry):
                here = first + t

                @pl.when(record_of(ids, here - 1) != ids[here])
                def _():
                    pick = picks[ids[here]]
                    for part in range(2):
                        spread(small, 0, entry[pick, part, 8 * group : 8 * group + 8, :])
                        for m in range(8):
                            states[part, m] = row(small, 0, m)

                re = [states[0, m] for m in range(8)]
                im = [states[1, m] for m in range(8)]
                value = product[8 * b + t]
                emit(8 * b + t, value, step(value, re, im))
                for m in range(8):
                    states[0, m] = re[m]
                    states[1, m] = im[m]
                return carry

            lax.fori_loop(0, 8, one, 0)

        return carry

    lax.fori_loop(0, ROWS // 8, block, 0)


def final_kernel(ids, picks, streams, border, taps, pole, entry, final_out, product_out, edge, states, small):
    position = first_position()
    for i in (1, 2):
        spread(edge, i * BLOCK, border[i].astype(F32))

    def emit(b, outs):
        for t in range(8):
            product_out[8 * b + t] = (outs[0][t] * outs[1][t]).astype(BF16).astype(F32)

    featurize(position, ids, (1, 2), streams, edge, taps, emit)
    for group in range(2):

        def step(value, re, im, group=group):
            for m in range(8):
                pr, pi = pole[0, 8 * group + m], pole[1, 8 * group + m]
                re[m], im[m] = pr * re[m] - pi * im[m] + value, pr * im[m] + pi * re[m]

        run_modes(
            position, ids, picks, entry, states, small, product_out, group, step, lambda at, value, out: None
        )
        for part in range(2):
            for m in range(0, 8, 2):
                pair = jnp.concatenate([states[part, m], states[part, m + 1]], axis=0)
                at = 64 * group + 8 * m
                final_out[part, at : at + 16, :] = pair.astype(BF16)


def final_states(ids, picks, streams, border, taps, pole, entry):
    return call(
        final_kernel,
        (
            jax.ShapeDtypeStruct((2, MODES * 8, LANES), BF16),
            jax.ShapeDtypeStruct((ROWS,) + WIDE, F32),
        ),
        [SMEM_SPEC] * 2 + [VMEM_SPEC] * 5,
        [
            pltpu.VMEM((3 * BLOCK, LANES), F32),
            pltpu.VMEM((2, 8) + WIDE, F32),
            pltpu.VMEM((BLOCK, LANES), F32),
        ],
        16,
        "final_states",
        8_000_000,
    )(ids, picks, streams, border, taps, pole, entry)


def query_kernel(ids, streams, border, taps, query_out, edge):
    spread(edge, 0, border[0].astype(F32))

    def emit(b, outs):
        for t in range(8):
            query_out[8 * b + t] = outs[0][t]

    featurize(first_position(), ids, (0,), streams, edge, taps, emit)


def featured_query(ids, streams, border, taps):
    return call(
        query_kernel,
        jax.ShapeDtypeStruct((ROWS,) + WIDE, F32),
        [SMEM_SPEC] + [VMEM_SPEC] * 3,
        [pltpu.VMEM((BLOCK, LANES), F32)],
        16,
        "featured_query",
        2_000_000,
    )(ids, streams, border, taps)


def residue_tables(res, tables, small, halves):
    for part in range(2):
        for half in halves:
            spread(small, 0, res[part, 8 * half : 8 * half + 8, :])
            for r in range(8):
                tables[part, 8 * half + r] = row(small, 0, r)


def modal_kernel(
    ids, picks, near, two, four, six, power, pole, res, skip, entry, product, query,
    gated_out, tables, carry_in, states, base, stage, small,
):
    for pair in range(MODES // 2):
        rows = slice(16 * pair, 16 * pair + 16)
        re, im = near[0, rows, :], near[1, rows, :]
        for n, ref in ((1, two), (2, four), (3, six)):
            other_re, other_im = ref[0, rows, :].astype(F32), ref[1, rows, :].astype(F32)
            power_re, power_im = power[n, 0, rows, :], power[n, 1, rows, :]
            re = re + power_re * other_re - power_im * other_im
            im = im + power_re * other_im + power_im * other_re
        for part, value in enumerate((re, im)):
            carry_in[part, 2 * pair] = value[:8]
            carry_in[part, 2 * pair + 1] = value[8:]

    residue_tables(res, tables, small, (0, 1))
    spread(small, 0, skip[...])
    skip_row = row(small, 0, 0)
    for group in range(2):

        def step(value, re, im, group=group):
            out = None
            for m in range(8):
                mode = 8 * group + m
                pr, pi = pole[0, mode], pole[1, mode]
                new_re = pr * re[m] - pi * im[m] + value
                new_im = pr * im[m] + pi * re[m]
                re[m], im[m] = new_re, new_im
                term = tables[0, mode] * new_re - tables[1, mode] * new_im
                out = term if out is None else out + term
            return out

        def emit(at, value, out, group=group):
            if group == 0:
                base[at] = skip_row * value + out
            else:
                value = query[at] * (base[at] + out)
                stage[pl.ds(at // 8 * BLOCK + at % 8, TILES, stride=GAP), :] = value

        run_modes(first_position(), ids, picks, entry, states, small, product, group, step, emit, carry_in)

    def gather(b, carry):
        for j in range(TILES):
            low = stage[pl.ds(2 * b * BLOCK + j * GAP, 8), :]
            high = stage[pl.ds((2 * b + 1) * BLOCK + j * GAP, 8), :]
            both = jnp.concatenate([low, high], axis=0).astype(BF16)
            gated_out[pl.ds(pl.multiple_of(16 * b, 16), 16), j * LANES : (j + 1) * LANES] = both
        return carry

    lax.fori_loop(0, ROWS // 16, gather, 0)


def gated_rows(ids, picks, near, two, four, six, power, pole, res, skip, entry, product, query):
    return call(
        modal_kernel,
        jax.ShapeDtypeStruct((ROWS, CH), BF16),
        [SMEM_SPEC] * 2 + [VMEM_SPEC] * 11,
        [
            pltpu.VMEM((2, MODES) + WIDE, F32),
            pltpu.VMEM((2, MODES) + WIDE, F32),
            pltpu.VMEM((2, 8) + WIDE, F32),
            pltpu.VMEM((ROWS,) + WIDE, F32),
            pltpu.VMEM((ROWS // 8 * BLOCK, LANES), F32),
            pltpu.VMEM((BLOCK, LANES), F32),
        ],
        20,
        "gated_rows",
        12_000_000,
    )(ids, picks, near, two, four, six, power, pole, res, skip, entry, product, query)


def partial_products(blocks, places, weights, name):
    rows = sum(part.stop - part.start for place in places for part, core in place) // 2

    def kernel(*refs):
        block_refs, weight_refs = refs[: len(blocks)], refs[len(blocks) : -2]
        out_ref, all_rows = refs[-2:]
        y, x = lax.axis_index("y"), lax.axis_index("x")
        zl, core = lax.axis_index("zl"), lax.axis_index("core")
        at = [0, rows]
        for ref, place in zip(block_refs, places):
            for part, owner in place:
                count = part.stop - part.start
                all_rows[at[owner] : at[owner] + count] = ref[part, :]
                at[owner] += count
        for which in range(2):
            own_y, next_y, last_y = [ref[which] for ref in weight_refs[:3]]
            for shift, weight in enumerate((own_y, next_y, weight_refs[3 + which][...], last_y)):
                slot = (y + shift - x + 4) % 4
                to = pl.multiple_of((zl + which) % 2 * COLS, COLS)
                part = jnp.dot(all_rows[...], weight, preferred_element_type=F32).astype(BF16)
                out_ref[core, slot, :, pl.ds(to, COLS)] = part[:rows]
                out_ref[1 - core, slot, :, pl.ds(to, COLS)] = part[rows:]

    return call(
        kernel,
        jax.ShapeDtypeStruct((2, 4, rows, 2 * COLS), BF16),
        [VMEM_SPEC] * (len(blocks) + 5),
        [pltpu.VMEM((2 * rows, CH), BF16)],
        24,
        name,
        1_000_000_000,
    )(*blocks, *weights)


def assemble_kernel(near_own, near_other, far_top, far_bottom, side, out_ref):
    zh, core = lax.axis_index("zh"), lax.axis_index("core")
    half = ROWS // 2
    same = pl.ds(pl.multiple_of(zh % 2 * 2 * COLS, 2 * COLS), 2 * COLS)
    other = pl.ds(pl.multiple_of((zh + 1) % 2 * 2 * COLS, 2 * COLS), 2 * COLS)

    @pl.when(zh // 2 == core)
    def _():
        out_ref[pl.ds(pl.multiple_of(core * half, half), half), same] = near_own[...]
        out_ref[pl.ds(pl.multiple_of((1 - core) * half, half), half), same] = near_other[...]

    @pl.when(zh // 2 != core)
    def _():
        out_ref[:half, same] = far_top[...]
        out_ref[half:, same] = far_bottom[...]

    out_ref[:, other] = side[...]


def add_complex(own, other, power):
    other = other.astype(F32)
    re = power[0] * other[0] - power[1] * other[1]
    im = power[0] * other[1] + power[1] * other[0]
    return own.astype(F32) + jnp.stack([re, im])


def shift_records(value, steps):
    return lax.ppermute(value, ("y", "zh", "zl"), [(i, i + steps) for i in range(32 - steps)])


def turn(value, axis, steps):
    return lax.ppermute(value, axis, [(i, (i + steps) % 4) for i in range(4)])


def tie(*values):
    return lax.optimization_barrier(values)


def shards(
    features, short_filter, decay, angle_rate, residues, skip, entry_states, segment_ids, state_ids, out_weight
):
    skip_row = skip.reshape(1, CH)
    pole, power, taps, streams, edge = prepare(
        segment_ids, features, short_filter.transpose(1, 0, 2), decay, angle_rate
    )
    power = power.reshape(4, 2, MODES * 8, LANES)
    border = shift_records(edge, 1)
    border, out_weight = tie(border, out_weight)
    paired = lax.ppermute(out_weight, "zl", [(0, 1), (1, 0)])
    final, product = final_states(segment_ids, state_ids, streams, border, taps, pole, entry_states)

    final, product = tie(final, product)
    last = shift_records(final, 1), shift_records(final, 2)
    query = featured_query(segment_ids, streams, border, taps)
    last, query, product, paired = tie(last, query, product, paired)
    near = add_complex(last[0], last[1], power[0])
    sent = near.astype(BF16)
    here = jnp.stack([out_weight, paired])
    lower, upper = turn(here, "y", 1), turn(here, "y", -1)
    gated = gated_rows(
        segment_ids, state_ids, near, *[shift_records(sent, steps) for steps in (2, 4, 6)],
        power, pole, residues, skip_row, entry_states, product, query,
    )

    gated, lower, upper = tie(gated, lower, upper)
    after, before = turn(gated, "zh", -1), turn(gated, "zh", 1)
    across, paired_across = turn(lower[0], "y", 1), turn(upper[1], "y", -1)
    weights = (here, upper, lower, across, paired_across)
    half = ROWS // 2
    top, bottom, whole = slice(0, half), slice(half, ROWS), slice(0, ROWS)
    after, before, weights = tie(after, before, weights)
    far = turn(after[top], "zh", -1), turn(before[bottom], "zh", 1)

    def over_cores(parts):
        other = lax.ppermute(parts[1], "core", [(0, 1), (1, 0)])
        return (parts[0].astype(F32) + other.astype(F32)).astype(BF16)

    def from_x(both, k):
        return turn(both[k], "x", k)

    def home(sums, moves):
        pairs = [(2 * zh + core, 2 * ((zh + step) % 4) + zh // 2) for zh in range(4) for core, step in moves]
        return lax.ppermute(sums, ("zh", "core"), pairs)

    def add(values):
        total = values[0].astype(F32)
        for value in values[1:]:
            total = total + value.astype(F32)
        return total.astype(BF16)

    places = [[(top, 0), (bottom, 1)], [(whole, 0)], [(whole, 1)]]
    one = over_cores(partial_products([gated, after, before], places, weights, "products_near"))
    one_1, one_3 = from_x(one, 1), from_x(one, 3)
    far, one, one_1, one_3 = tie(far, one, one_1, one_3)
    two = over_cores(partial_products(far, [[(top, 0)], [(top, 1)]], weights, "products_far"))
    one = add([one[0], one_1, from_x(one, 2), one_3])
    two = add([two[0]] + [from_x(two, k) for k in range(1, 4)])
    near_own = one[:half]
    near_other = lax.ppermute(near_own, "core", [(0, 1), (1, 0)])
    side = home(one[half:], [(0, 1), (1, 3)])
    far_top, far_bottom = home(two, [(0, 2)]), home(two, [(1, 2)])
    return call(
        assemble_kernel, jax.ShapeDtypeStruct((ROWS, CH), BF16), [VMEM_SPEC] * 5, [], 8, "assemble", 1_000_000
    )(near_own, near_other, far_top, far_bottom, side)


def solution(mesh):
    fine = Mesh(mesh.devices.reshape(4, 4, 2, 4, 2), ("y", "zh", "zl", "x", "core"))
    seq, chan = ("y", "zh", "zl"), ("x", "core")
    in_specs = (
        P(None, seq, chan),
        P(None, None, chan),
        P(None, chan),
        P(None, chan),
        P(None, None, chan),
        P(chan),
        P(None, None, None, chan),
        P(),
        P(),
        P(chan, seq),
    )
    return jax.shard_map(shards, mesh=fine, in_specs=in_specs, out_specs=P(seq, chan), check_vma=False)
```

```python
import jax
import jax.numpy as jnp
from jax import lax
from jax.experimental import pallas as pl
from jax.experimental.pallas import tpu as pltpu
from jax.sharding import Mesh
from jax.sharding import PartitionSpec as P

F32 = jnp.float32
BF16 = jnp.bfloat16
ROWS = 256
CH = 1024
LANES = 128
TILES = CH // LANES
MODES = 16
TAPS = 7
GROUP = 16
GAP = 9
BLOCK = GAP * TILES
COLS = 256
WIDE = (8, LANES)
MIB = 1024 * 1024
SMEM_SPEC = pl.BlockSpec(memory_space=pltpu.SMEM)
VMEM_SPEC = pl.BlockSpec(memory_space=pltpu.VMEM)


def call(kernel, outs, in_specs, scratch, limit, name, cycles, interpret=False):
    return pl.pallas_call(
        kernel,
        out_shape=outs,
        in_specs=in_specs,
        out_specs=jax.tree.map(lambda out: VMEM_SPEC, outs),
        scratch_shapes=scratch,
        compiler_params=pltpu.CompilerParams(vmem_limit_bytes=limit * MIB),
        cost_estimate=pl.CostEstimate(flops=cycles, transcendentals=0, bytes_accessed=MIB),
        name=name,
        interpret=interpret,
    )


def first_position():
    device = (lax.axis_index("y") * 4 + lax.axis_index("zh")) * 2 + lax.axis_index("zl")
    return device * ROWS


def spread(scratch, base, value):
    for j in range(TILES):
        scratch[pl.ds(base + j * GAP, value.shape[0]), :] = value[:, j * LANES : (j + 1) * LANES]


def row(scratch, base, r):
    return scratch[pl.ds(base + r, TILES, stride=GAP), :]


def record_of(ids, position):
    return jnp.where(position < 0, -1, ids[jnp.maximum(position, 0)])


def prepare_kernel(ids, filt, decay, angle, pole_out, power_out, taps_out, small):
    position = first_position()
    for half in range(2):
        rows = slice(8 * half, 8 * half + 8)
        mag = jnp.exp(-decay[rows, :])
        ang = angle[rows, :]
        spread(small, 0, mag * jnp.cos(ang))
        spread(small, BLOCK, mag * jnp.sin(ang))
        for r in range(8):
            pole_out[0, 0, 8 * half + r] = row(small, 0, r)
            pole_out[0, 1, 8 * half + r] = row(small, BLOCK, r)
    keeps = []
    for count, last in ((1, position + ROWS - 1), (2, position + ROWS - 1), (3, position + ROWS - 1), (4, position - 1)):
        before = last - count * ROWS
        keeps.append(jnp.where((before >= 0) & (record_of(ids, before) == record_of(ids, last)), 1.0, 0.0))
    for m in range(MODES):
        re, im = pole_out[0, 0, m], pole_out[0, 1, m]
        two_re, two_im = re * re - im * im, 2.0 * re * im
        pole_out[1, 0, m], pole_out[1, 1, m] = two_re, two_im
        pole_out[2, 0, m], pole_out[2, 1, m] = re * two_re - im * two_im, re * two_im + im * two_re
        re, im = two_re * two_re - two_im * two_im, 2.0 * two_re * two_im
        pole_out[3, 0, m], pole_out[3, 1, m] = re, im
        for doubling in range(6):
            re, im = re * re - im * im, 2.0 * re * im
        two_re, two_im = re * re - im * im, 2.0 * re * im
        powers = (
            (re, im),
            (two_re, two_im),
            (re * two_re - im * two_im, re * two_im + im * two_re),
            (two_re * two_re - two_im * two_im, 2.0 * two_re * two_im),
        )
        for n in range(4):
            power_out[n, 0, m] = powers[n][0] * keeps[n]
            power_out[n, 1, m] = powers[n][1] * keeps[n]
    groups = CH // GROUP
    group = lax.broadcasted_iota(jnp.int32, (groups, CH), 0)
    channel = lax.broadcasted_iota(jnp.int32, (groups, CH), 1)
    widen = jnp.where(channel // GROUP == group, 1.0, 0.0).astype(BF16)
    for i in range(3):
        spread(small, 0, jnp.dot(filt[i], widen, preferred_element_type=F32))
        for j in range(TAPS):
            taps_out[j, i] = row(small, 0, j)


def prepare(ids, filt, decay, angle):
    return call(
        prepare_kernel,
        (
            jax.ShapeDtypeStruct((4, 2, MODES) + WIDE, F32),
            jax.ShapeDtypeStruct((4, 2, MODES) + WIDE, F32),
            jax.ShapeDtypeStruct((TAPS, 3) + WIDE, F32),
        ),
        [SMEM_SPEC] + [VMEM_SPEC] * 3,
        [pltpu.VMEM((2 * BLOCK, LANES), F32)],
        58,
        "prepare",
        3_000_000,
    )(ids, filt, decay, angle)


def lay_out(feat, which, streams):
    def step(b, carry):
        for n, i in enumerate(which):
            value = feat[i, pl.ds(pl.multiple_of(b * 16, 16), 16), :].astype(F32)
            spread(streams.at[n], 2 * b * BLOCK, value[:8])
            spread(streams.at[n], (2 * b + 1) * BLOCK, value[8:])
        return carry

    lax.fori_loop(0, ROWS // 16, step, 0)


def featurized(values, taps, same):
    outs = []
    for t in range(8):
        out = taps[0] * values[6 + t]
        for j in range(1, TAPS):
            value = values[6 + t - j]
            if same is not None:
                value = jnp.where(same[t][j], value, 0.0)
            out = out + taps[j] * value
        outs.append(out)
    return outs


def featurize(position, ids, which, streams, edge, taps, emit):
    def step(b, before):
        first = position + 8 * b
        plain = record_of(ids, first - 6) == ids[first + 7]
        rows = [[row(streams.at[n], b * BLOCK, r) for r in range(8)] for n in range(len(which))]

        def run(same):
            emit(
                b,
                [
                    featurized([*before[n], *rows[n]], [taps[j, i] for j in range(TAPS)], same)
                    for n, i in enumerate(which)
                ],
            )

        @pl.when(plain)
        def _():
            run(None)

        @pl.when(jnp.logical_not(plain))
        def _():
            run([[record_of(ids, first + t - j) == ids[first + t] for j in range(TAPS)] for t in range(8)])

        return tuple(tuple(eight[2:]) for eight in rows)

    lax.fori_loop(0, ROWS // 8, step, tuple(tuple(row(edge, i * BLOCK, 2 + r) for r in range(6)) for i in which))


def run_modes(position, ids, picks, entry, states, small, product, group, step, emit, carry_in=None, block_step=None):
    for part in range(2):
        for m in range(8):
            states[part, m] = jnp.zeros(WIDE, F32) if carry_in is None else carry_in[part, 8 * group + m]

    def block(b, carry):
        first = position + 8 * b
        plain = record_of(ids, first - 1) == ids[first + 7]

        @pl.when(plain)
        def _():
            re = [states[0, m] for m in range(8)]
            im = [states[1, m] for m in range(8)]
            if block_step is None:
                for t in range(8):
                    value = product[8 * b + t]
                    emit(8 * b + t, value, step(value, re, im))
            else:
                block_step([product[8 * b + t] for t in range(8)], re, im)
            for m in range(8):
                states[0, m] = re[m]
                states[1, m] = im[m]

        @pl.when(jnp.logical_not(plain))
        def _():
            def one(t, carry):
                here = first + t

                @pl.when(record_of(ids, here - 1) != ids[here])
                def _():
                    pick = picks[ids[here]]
                    for part in range(2):
                        spread(small, 0, entry[pick, part, 8 * group : 8 * group + 8, :])
                        for m in range(8):
                            states[part, m] = row(small, 0, m)

                re = [states[0, m] for m in range(8)]
                im = [states[1, m] for m in range(8)]
                value = product[8 * b + t]
                emit(8 * b + t, value, step(value, re, im))
                for m in range(8):
                    states[0, m] = re[m]
                    states[1, m] = im[m]
                return carry

            lax.fori_loop(0, 8, one, 0)

        return carry

    lax.fori_loop(0, ROWS // 8, block, 0)


def final_kernel(ids, picks, feat, border, taps, pole, entry, final_out, product_out, streams, edge, states, small):
    position = first_position()
    lay_out(feat, (1, 2), streams)
    for i in (1, 2):
        spread(edge, i * BLOCK, border[i].astype(F32))

    def emit(b, outs):
        for t in range(8):
            product_out[8 * b + t] = (outs[0][t] * outs[1][t]).astype(BF16).astype(F32)

    featurize(position, ids, (1, 2), streams, edge, taps, emit)
    for group in range(2):

        def step(value, re, im, group=group):
            for m in range(8):
                pr, pi = pole[0, 0, 8 * group + m], pole[0, 1, 8 * group + m]
                re[m], im[m] = pr * re[m] - pi * im[m] + value, pr * im[m] + pi * re[m]

        def block_step(values, re, im, group=group):
            for m in range(8):
                power_re = [pole[n, 0, 8 * group + m] for n in range(4)]
                power_im = [pole[n, 1, 8 * group + m] for n in range(4)]
                for at in (0, 4):
                    first, second, third, fourth = values[at : at + 4]
                    new_re = power_re[2] * first + power_re[1] * second + power_re[0] * third + fourth
                    new_im = power_im[2] * first + power_im[1] * second + power_im[0] * third
                    re[m], im[m] = (
                        power_re[3] * re[m] - power_im[3] * im[m] + new_re,
                        power_re[3] * im[m] + power_im[3] * re[m] + new_im,
                    )

        run_modes(
            position, ids, picks, entry, states, small, product_out, group, step, lambda at, value, out: None,
            block_step=block_step,
        )
        for part in range(2):
            for m in range(0, 8, 2):
                pair = jnp.concatenate([states[part, m], states[part, m + 1]], axis=0)
                at = 64 * group + 8 * m
                final_out[part, at : at + 16, :] = pair.astype(BF16)


def final_states(ids, picks, feat, border, taps, pole, entry):
    return call(
        final_kernel,
        (
            jax.ShapeDtypeStruct((2, MODES * 8, LANES), BF16),
            jax.ShapeDtypeStruct((ROWS,) + WIDE, F32),
        ),
        [SMEM_SPEC] * 2 + [VMEM_SPEC] * 5,
        [
            pltpu.VMEM((2, ROWS // 8 * BLOCK, LANES), F32),
            pltpu.VMEM((3 * BLOCK, LANES), F32),
            pltpu.VMEM((2, 8) + WIDE, F32),
            pltpu.VMEM((BLOCK, LANES), F32),
        ],
        58,
        "final_states",
        8_000_000,
    )(ids, picks, feat, border, taps, pole, entry)


def query_kernel(ids, feat, border, taps, query_out, streams, edge):
    lay_out(feat, (0,), streams)
    spread(edge, 0, border[0].astype(F32))

    def emit(b, outs):
        for t in range(8):
            query_out[8 * b + t] = outs[0][t]

    featurize(first_position(), ids, (0,), streams, edge, taps, emit)


def featured_query(ids, feat, border, taps):
    return call(
        query_kernel,
        jax.ShapeDtypeStruct((ROWS,) + WIDE, F32),
        [SMEM_SPEC] + [VMEM_SPEC] * 3,
        [pltpu.VMEM((1, ROWS // 8 * BLOCK, LANES), F32), pltpu.VMEM((BLOCK, LANES), F32)],
        16,
        "featured_query",
        2_000_000,
    )(ids, feat, border, taps)


def residue_tables(res, tables, small, halves):
    for part in range(2):
        for half in halves:
            spread(small, 0, res[part, 8 * half : 8 * half + 8, :])
            for r in range(8):
                tables[part, 8 * half + r] = row(small, 0, r)


def modal_kernel(
    ids, picks, near, far, power, pole, res, skip, entry, product, query,
    gated_out, tables, carry_in, states, base, stage, small,
):
    for pair in range(MODES // 2):
        rows = slice(16 * pair, 16 * pair + 16)
        far_re, far_im = far[0, rows, :].astype(F32), far[1, rows, :].astype(F32)
        power_re, power_im = power[3, 0, rows, :], power[3, 1, rows, :]
        re = near[0, rows, :].astype(F32) + power_re * far_re - power_im * far_im
        im = near[1, rows, :].astype(F32) + power_re * far_im + power_im * far_re
        for part, value in enumerate((re, im)):
            carry_in[part, 2 * pair] = value[:8]
            carry_in[part, 2 * pair + 1] = value[8:]

    residue_tables(res, tables, small, (0, 1))
    spread(small, 0, skip[...])
    skip_row = row(small, 0, 0)
    for group in range(2):

        def step(value, re, im, group=group):
            out = None
            for m in range(8):
                mode = 8 * group + m
                pr, pi = pole[0, 0, mode], pole[0, 1, mode]
                new_re = pr * re[m] - pi * im[m] + value
                new_im = pr * im[m] + pi * re[m]
                re[m], im[m] = new_re, new_im
                term = tables[0, mode] * new_re - tables[1, mode] * new_im
                out = term if out is None else out + term
            return out

        def emit(at, value, out, group=group):
            if group == 0:
                base[at] = skip_row * value + out
            else:
                value = query[at] * (base[at] + out)
                stage[pl.ds(at // 8 * BLOCK + at % 8, TILES, stride=GAP), :] = value

        run_modes(first_position(), ids, picks, entry, states, small, product, group, step, emit, carry_in)

    def gather(b, carry):
        for j in range(TILES):
            low = stage[pl.ds(2 * b * BLOCK + j * GAP, 8), :]
            high = stage[pl.ds((2 * b + 1) * BLOCK + j * GAP, 8), :]
            both = jnp.concatenate([low, high], axis=0).astype(BF16)
            gated_out[pl.ds(pl.multiple_of(16 * b, 16), 16), j * LANES : (j + 1) * LANES] = both
        return carry

    lax.fori_loop(0, ROWS // 16, gather, 0)


def gated_rows(ids, picks, near, far, power, pole, res, skip, entry, product, query):
    return call(
        modal_kernel,
        jax.ShapeDtypeStruct((ROWS, CH), BF16),
        [SMEM_SPEC] * 2 + [VMEM_SPEC] * 9,
        [
            pltpu.VMEM((2, MODES) + WIDE, F32),
            pltpu.VMEM((2, MODES) + WIDE, F32),
            pltpu.VMEM((2, 8) + WIDE, F32),
            pltpu.VMEM((ROWS,) + WIDE, F32),
            pltpu.VMEM((ROWS // 8 * BLOCK, LANES), F32),
            pltpu.VMEM((BLOCK, LANES), F32),
        ],
        20,
        "gated_rows",
        12_000_000,
    )(ids, picks, near, far, power, pole, res, skip, entry, product, query)


def partial_products(blocks, places, weights, name):
    rows = sum(part.stop - part.start for place in places for part, core in place) // 2

    def kernel(*refs):
        block_refs, weight_refs = refs[: len(blocks)], refs[len(blocks) : -2]
        out_ref, all_rows = refs[-2:]
        y, x = lax.axis_index("y"), lax.axis_index("x")
        zl, core = lax.axis_index("zl"), lax.axis_index("core")
        at = [0, rows]
        for ref, place in zip(block_refs, places):
            for part, owner in place:
                count = part.stop - part.start
                all_rows[at[owner] : at[owner] + count] = ref[part, :]
                at[owner] += count
        for which in range(2):
            own_y, next_y, last_y = [ref[which] for ref in weight_refs[:3]]
            for shift, weight in enumerate((own_y, next_y, weight_refs[3 + which][...], last_y)):
                slot = (y + shift - x + 4) % 4
                to = pl.multiple_of((zl + which) % 2 * COLS, COLS)
                part = jnp.dot(all_rows[...], weight, preferred_element_type=F32).astype(BF16)
                out_ref[core, slot, :, pl.ds(to, COLS)] = part[:rows]
                out_ref[1 - core, slot, :, pl.ds(to, COLS)] = part[rows:]

    return call(
        kernel,
        jax.ShapeDtypeStruct((2, 4, rows, 2 * COLS), BF16),
        [VMEM_SPEC] * (len(blocks) + 5),
        [pltpu.VMEM((2 * rows, CH), BF16)],
        24,
        name,
        1_000_000_000,
    )(*blocks, *weights)


def assemble_kernel(near_own, near_other, far_top, far_bottom, side, out_ref):
    zh, core = lax.axis_index("zh"), lax.axis_index("core")
    half = ROWS // 2
    same = pl.ds(pl.multiple_of(zh % 2 * 2 * COLS, 2 * COLS), 2 * COLS)
    other = pl.ds(pl.multiple_of((zh + 1) % 2 * 2 * COLS, 2 * COLS), 2 * COLS)

    @pl.when(zh // 2 == core)
    def _():
        out_ref[pl.ds(pl.multiple_of(core * half, half), half), same] = near_own[...]
        out_ref[pl.ds(pl.multiple_of((1 - core) * half, half), half), same] = near_other[...]

    @pl.when(zh // 2 != core)
    def _():
        out_ref[:half, same] = far_top[...]
        out_ref[half:, same] = far_bottom[...]

    out_ref[:, other] = side[...]


def add_complex(own, other, power):
    other = other.astype(F32)
    re = power[0] * other[0] - power[1] * other[1]
    im = power[0] * other[1] + power[1] * other[0]
    return own.astype(F32) + jnp.stack([re, im])


def shift_records(value, steps):
    return lax.ppermute(value, ("y", "zh", "zl"), [(i, i + steps) for i in range(32 - steps)])


def turn(value, axis, steps):
    return lax.ppermute(value, axis, [(i, (i + steps) % 4) for i in range(4)])


def tie(*values):
    return lax.optimization_barrier(values)


def shards(
    features, short_filter, decay, angle_rate, residues, skip, entry_states, segment_ids, state_ids, out_weight
):
    skip_row = skip.reshape(1, CH)
    border = shift_records(features[:, ROWS - 8 :, :], 1)
    pole, power, taps = prepare(segment_ids, short_filter.transpose(1, 0, 2), decay, angle_rate)
    power = power.reshape(4, 2, MODES * 8, LANES)
    border, out_weight, pole = tie(border, out_weight, pole)
    paired = lax.ppermute(out_weight, "zl", [(0, 1), (1, 0)])
    final, product = final_states(segment_ids, state_ids, features, border, taps, pole, entry_states)

    final, product = tie(final, product)
    last = [shift_records(final, steps) for steps in (3, 2, 1)][::-1]
    query = featured_query(segment_ids, features, border, taps)
    last, query, product, paired = tie(last, query, product, paired)
    leaving = final
    for n in range(3):
        leaving = add_complex(leaving, last[n], power[n])
    leaving = leaving.astype(BF16)
    entering = [shift_records(leaving, steps) for steps in (5, 1)][::-1]
    entering, out_weight, paired = tie(entering, out_weight, paired)
    here = jnp.stack([out_weight, paired])
    lower, upper = turn(here, "y", 1), turn(here, "y", -1)
    gated = gated_rows(
        segment_ids, state_ids, *entering, power, pole, residues, skip_row, entry_states, product, query
    )

    after, before = turn(gated, "zh", -1), turn(gated, "zh", 1)
    across, paired_across = turn(lower[0], "y", 1), turn(upper[1], "y", -1)
    weights = (here, upper, lower, across, paired_across)
    half = ROWS // 2
    top, bottom, whole = slice(0, half), slice(half, ROWS), slice(0, ROWS)
    after, before, weights = tie(after, before, weights)
    far = turn(after[top], "zh", -1), turn(before[bottom], "zh", 1)

    def over_cores(parts):
        other = lax.ppermute(parts[1], "core", [(0, 1), (1, 0)])
        return (parts[0].astype(F32) + other.astype(F32)).astype(BF16)

    def from_x(both, k):
        return turn(both[k], "x", k)

    def home(sums, moves):
        pairs = [(2 * zh + core, 2 * ((zh + step) % 4) + zh // 2) for zh in range(4) for core, step in moves]
        return lax.ppermute(sums, ("zh", "core"), pairs)

    def add(values):
        total = values[0].astype(F32)
        for value in values[1:]:
            total = total + value.astype(F32)
        return total.astype(BF16)

    places = [[(top, 0), (bottom, 1)], [(whole, 0)], [(whole, 1)]]
    one = over_cores(partial_products([gated, after, before], places, weights, "products_near"))
    one_x = [from_x(one, k) for k in (2, 1, 3)]
    far, one, one_x = tie(far, one, one_x)
    two = over_cores(partial_products(far, [[(top, 0)], [(top, 1)]], weights, "products_far"))
    one = add([one[0], *one_x])
    two = add([two[0]] + [from_x(two, k) for k in range(1, 4)])
    near_own = one[:half]
    near_other = lax.ppermute(near_own, "core", [(0, 1), (1, 0)])
    side = home(one[half:], [(0, 1), (1, 3)])
    far_top, far_bottom = home(two, [(0, 2)]), home(two, [(1, 2)])
    return call(
        assemble_kernel, jax.ShapeDtypeStruct((ROWS, CH), BF16), [VMEM_SPEC] * 5, [], 8, "assemble", 1_000_000
    )(near_own, near_other, far_top, far_bottom, side)


def solution(mesh):
    fine = Mesh(mesh.devices.reshape(4, 4, 2, 4, 2), ("y", "zh", "zl", "x", "core"))
    seq, chan = ("y", "zh", "zl"), ("x", "core")
    in_specs = (
        P(None, seq, chan),
        P(None, None, chan),
        P(None, chan),
        P(None, chan),
        P(None, None, chan),
        P(chan),
        P(None, None, None, chan),
        P(),
        P(),
        P(chan, seq),
    )
    return jax.shard_map(shards, mesh=fine, in_specs=in_specs, out_specs=P(seq, chan), check_vma=False)
```

```python
import jax
import jax.numpy as jnp
from jax import lax
from jax.experimental import pallas as pl
from jax.experimental.pallas import tpu as pltpu
from jax.sharding import Mesh
from jax.sharding import PartitionSpec as P

F32 = jnp.float32
BF16 = jnp.bfloat16
ROWS = 256
CH = 1024
LANES = 128
TILES = CH // LANES
MODES = 16
TAPS = 7
GROUP = 16
GAP = 9
BLOCK = GAP * TILES
COLS = 256
WIDE = (8, LANES)
MIB = 1024 * 1024
SMEM_SPEC = pl.BlockSpec(memory_space=pltpu.SMEM)
VMEM_SPEC = pl.BlockSpec(memory_space=pltpu.VMEM)


def call(kernel, outs, in_specs, scratch, limit, name, cycles, interpret=False):
    return pl.pallas_call(
        kernel,
        out_shape=outs,
        in_specs=in_specs,
        out_specs=jax.tree.map(lambda out: VMEM_SPEC, outs),
        scratch_shapes=scratch,
        compiler_params=pltpu.CompilerParams(vmem_limit_bytes=limit * MIB),
        cost_estimate=pl.CostEstimate(flops=cycles, transcendentals=0, bytes_accessed=MIB),
        name=name,
        interpret=interpret,
    )


def first_position():
    device = (lax.axis_index("y") * 4 + lax.axis_index("zh")) * 2 + lax.axis_index("zl")
    return device * ROWS


def spread(scratch, base, value):
    for j in range(TILES):
        scratch[pl.ds(base + j * GAP, value.shape[0]), :] = value[:, j * LANES : (j + 1) * LANES]


def row(scratch, base, r):
    return scratch[pl.ds(base + r, TILES, stride=GAP), :]


def record_of(ids, position):
    return jnp.where(position < 0, -1, ids[jnp.maximum(position, 0)])


def prepare_kernel(ids, filt, decay, angle, pole_out, power_out, taps_out, small):
    position = first_position()
    for half in range(2):
        rows = slice(8 * half, 8 * half + 8)
        mag = jnp.exp(-decay[rows, :])
        ang = angle[rows, :]
        spread(small, 0, mag * jnp.cos(ang))
        spread(small, BLOCK, mag * jnp.sin(ang))
        for r in range(8):
            pole_out[0, 0, 8 * half + r] = row(small, 0, r)
            pole_out[0, 1, 8 * half + r] = row(small, BLOCK, r)
    keeps = []
    for count, last in ((1, position + ROWS - 1), (2, position + ROWS - 1), (3, position + ROWS - 1), (4, position - 1)):
        before = last - count * ROWS
        keeps.append(jnp.where((before >= 0) & (record_of(ids, before) == record_of(ids, last)), 1.0, 0.0))
    for m in range(MODES):
        re, im = pole_out[0, 0, m], pole_out[0, 1, m]
        two_re, two_im = re * re - im * im, 2.0 * re * im
        pole_out[1, 0, m], pole_out[1, 1, m] = two_re, two_im
        pole_out[2, 0, m], pole_out[2, 1, m] = re * two_re - im * two_im, re * two_im + im * two_re
        re, im = two_re * two_re - two_im * two_im, 2.0 * two_re * two_im
        pole_out[3, 0, m], pole_out[3, 1, m] = re, im
        for doubling in range(6):
            re, im = re * re - im * im, 2.0 * re * im
        two_re, two_im = re * re - im * im, 2.0 * re * im
        powers = (
            (re, im),
            (two_re, two_im),
            (re * two_re - im * two_im, re * two_im + im * two_re),
            (two_re * two_re - two_im * two_im, 2.0 * two_re * two_im),
        )
        for n in range(4):
            power_out[n, 0, m] = powers[n][0] * keeps[n]
            power_out[n, 1, m] = powers[n][1] * keeps[n]
    groups = CH // GROUP
    group = lax.broadcasted_iota(jnp.int32, (groups, CH), 0)
    channel = lax.broadcasted_iota(jnp.int32, (groups, CH), 1)
    widen = jnp.where(channel // GROUP == group, 1.0, 0.0).astype(BF16)
    for i in range(3):
        spread(small, 0, jnp.dot(filt[i], widen, preferred_element_type=F32))
        for j in range(TAPS):
            taps_out[j, i] = row(small, 0, j)


def prepare(ids, filt, decay, angle):
    return call(
        prepare_kernel,
        (
            jax.ShapeDtypeStruct((4, 2, MODES) + WIDE, F32),
            jax.ShapeDtypeStruct((4, 2, MODES) + WIDE, F32),
            jax.ShapeDtypeStruct((TAPS, 3) + WIDE, F32),
        ),
        [SMEM_SPEC] + [VMEM_SPEC] * 3,
        [pltpu.VMEM((2 * BLOCK, LANES), F32)],
        58,
        "prepare",
        3_000_000,
    )(ids, filt, decay, angle)


def lay_out(feat, which, streams):
    def step(b, carry):
        for n, i in enumerate(which):
            value = feat[i, pl.ds(pl.multiple_of(b * 16, 16), 16), :].astype(F32)
            spread(streams.at[n], 2 * b * BLOCK, value[:8])
            spread(streams.at[n], (2 * b + 1) * BLOCK, value[8:])
        return carry

    lax.fori_loop(0, ROWS // 16, step, 0)


def featurized(values, taps, same):
    outs = []
    for t in range(8):
        out = taps[0] * values[6 + t]
        for j in range(1, TAPS):
            value = values[6 + t - j]
            if same is not None:
                value = jnp.where(same[t][j], value, 0.0)
            out = out + taps[j] * value
        outs.append(out)
    return outs


def featurize(position, ids, which, streams, edge, taps, emit):
    def step(b, before):
        first = position + 8 * b
        plain = record_of(ids, first - 6) == ids[first + 7]
        rows = [[row(streams.at[n], b * BLOCK, r) for r in range(8)] for n in range(len(which))]

        def run(same):
            emit(
                b,
                [
                    featurized([*before[n], *rows[n]], [taps[j, i] for j in range(TAPS)], same)
                    for n, i in enumerate(which)
                ],
            )

        @pl.when(plain)
        def _():
            run(None)

        @pl.when(jnp.logical_not(plain))
        def _():
            run([[record_of(ids, first + t - j) == ids[first + t] for j in range(TAPS)] for t in range(8)])

        return tuple(tuple(eight[2:]) for eight in rows)

    lax.fori_loop(0, ROWS // 8, step, tuple(tuple(row(edge, i * BLOCK, 2 + r) for r in range(6)) for i in which))


def run_modes(position, ids, picks, entry, states, small, product, group, step, emit, carry_in=None, block_step=None):
    for part in range(2):
        for m in range(8):
            states[part, m] = jnp.zeros(WIDE, F32) if carry_in is None else carry_in[part, 8 * group + m]

    def block(b, carry):
        first = position + 8 * b
        plain = record_of(ids, first - 1) == ids[first + 7]

        @pl.when(plain)
        def _():
            re = [states[0, m] for m in range(8)]
            im = [states[1, m] for m in range(8)]
            if block_step is None:
                for t in range(8):
                    value = product[8 * b + t]
                    emit(8 * b + t, value, step(value, re, im))
            else:
                block_step([product[8 * b + t] for t in range(8)], re, im)
            for m in range(8):
                states[0, m] = re[m]
                states[1, m] = im[m]

        @pl.when(jnp.logical_not(plain))
        def _():
            def one(t, carry):
                here = first + t

                @pl.when(record_of(ids, here - 1) != ids[here])
                def _():
                    pick = picks[ids[here]]
                    for part in range(2):
                        spread(small, 0, entry[pick, part, 8 * group : 8 * group + 8, :])
                        for m in range(8):
                            states[part, m] = row(small, 0, m)

                re = [states[0, m] for m in range(8)]
                im = [states[1, m] for m in range(8)]
                value = product[8 * b + t]
                emit(8 * b + t, value, step(value, re, im))
                for m in range(8):
                    states[0, m] = re[m]
                    states[1, m] = im[m]
                return carry

            lax.fori_loop(0, 8, one, 0)

        return carry

    lax.fori_loop(0, ROWS // 8, block, 0)


def final_kernel(ids, picks, feat, border, taps, pole, entry, final_out, product_out, streams, edge, states, small):
    position = first_position()
    lay_out(feat, (1, 2), streams)
    for i in (1, 2):
        spread(edge, i * BLOCK, border[i].astype(F32))

    def emit(b, outs):
        for t in range(8):
            product_out[8 * b + t] = (outs[0][t] * outs[1][t]).astype(BF16).astype(F32)

    featurize(position, ids, (1, 2), streams, edge, taps, emit)
    for group in range(2):

        def step(value, re, im, group=group):
            for m in range(8):
                pr, pi = pole[0, 0, 8 * group + m], pole[0, 1, 8 * group + m]
                re[m], im[m] = pr * re[m] - pi * im[m] + value, pr * im[m] + pi * re[m]

        def block_step(values, re, im, group=group):
            for m in range(8):
                power_re = [pole[n, 0, 8 * group + m] for n in range(4)]
                power_im = [pole[n, 1, 8 * group + m] for n in range(4)]
                for at in (0, 4):
                    first, second, third, fourth = values[at : at + 4]
                    new_re = power_re[2] * first + power_re[1] * second + power_re[0] * third + fourth
                    new_im = power_im[2] * first + power_im[1] * second + power_im[0] * third
                    re[m], im[m] = (
                        power_re[3] * re[m] - power_im[3] * im[m] + new_re,
                        power_re[3] * im[m] + power_im[3] * re[m] + new_im,
                    )

        run_modes(
            position, ids, picks, entry, states, small, product_out, group, step, lambda at, value, out: None,
            block_step=block_step,
        )
        for part in range(2):
            for m in range(0, 8, 2):
                pair = jnp.concatenate([states[part, m], states[part, m + 1]], axis=0)
                at = 64 * group + 8 * m
                final_out[part, at : at + 16, :] = pair.astype(BF16)


def final_states(ids, picks, feat, border, taps, pole, entry):
    return call(
        final_kernel,
        (
            jax.ShapeDtypeStruct((2, MODES * 8, LANES), BF16),
            jax.ShapeDtypeStruct((ROWS,) + WIDE, F32),
        ),
        [SMEM_SPEC] * 2 + [VMEM_SPEC] * 5,
        [
            pltpu.VMEM((2, ROWS // 8 * BLOCK, LANES), F32),
            pltpu.VMEM((3 * BLOCK, LANES), F32),
            pltpu.VMEM((2, 8) + WIDE, F32),
            pltpu.VMEM((BLOCK, LANES), F32),
        ],
        58,
        "final_states",
        8_000_000,
    )(ids, picks, feat, border, taps, pole, entry)


def query_kernel(ids, feat, border, taps, query_out, streams, edge):
    lay_out(feat, (0,), streams)
    spread(edge, 0, border[0].astype(F32))

    def emit(b, outs):
        for t in range(8):
            query_out[8 * b + t] = outs[0][t]

    featurize(first_position(), ids, (0,), streams, edge, taps, emit)


def featured_query(ids, feat, border, taps):
    return call(
        query_kernel,
        jax.ShapeDtypeStruct((ROWS,) + WIDE, F32),
        [SMEM_SPEC] + [VMEM_SPEC] * 3,
        [pltpu.VMEM((1, ROWS // 8 * BLOCK, LANES), F32), pltpu.VMEM((BLOCK, LANES), F32)],
        16,
        "featured_query",
        2_000_000,
    )(ids, feat, border, taps)


def residue_tables(res, tables, small, halves):
    for part in range(2):
        for half in halves:
            spread(small, 0, res[part, 8 * half : 8 * half + 8, :])
            for r in range(8):
                tables[part, 8 * half + r] = row(small, 0, r)


def modal_kernel(
    ids, picks, near, far, power, pole, res, skip, entry, product, query,
    gated_out, tables, carry_in, states, base, stage, small,
):
    for pair in range(MODES // 2):
        rows = slice(16 * pair, 16 * pair + 16)
        far_re, far_im = far[0, rows, :].astype(F32), far[1, rows, :].astype(F32)
        power_re, power_im = power[3, 0, rows, :], power[3, 1, rows, :]
        re = near[0, rows, :].astype(F32) + power_re * far_re - power_im * far_im
        im = near[1, rows, :].astype(F32) + power_re * far_im + power_im * far_re
        for part, value in enumerate((re, im)):
            carry_in[part, 2 * pair] = value[:8]
            carry_in[part, 2 * pair + 1] = value[8:]

    residue_tables(res, tables, small, (0, 1))
    spread(small, 0, skip[...])
    skip_row = row(small, 0, 0)
    for group in range(2):

        def step(value, re, im, group=group):
            out = None
            for m in range(8):
                mode = 8 * group + m
                pr, pi = pole[0, 0, mode], pole[0, 1, mode]
                new_re = pr * re[m] - pi * im[m] + value
                new_im = pr * im[m] + pi * re[m]
                re[m], im[m] = new_re, new_im
                term = tables[0, mode] * new_re - tables[1, mode] * new_im
                out = term if out is None else out + term
            return out

        def emit(at, value, out, group=group):
            if group == 0:
                base[at] = skip_row * value + out
            else:
                value = query[at] * (base[at] + out)
                stage[pl.ds(at // 8 * BLOCK + at % 8, TILES, stride=GAP), :] = value

        run_modes(first_position(), ids, picks, entry, states, small, product, group, step, emit, carry_in)

    def gather(b, carry):
        for j in range(TILES):
            low = stage[pl.ds(2 * b * BLOCK + j * GAP, 8), :]
            high = stage[pl.ds((2 * b + 1) * BLOCK + j * GAP, 8), :]
            both = jnp.concatenate([low, high], axis=0).astype(BF16)
            gated_out[pl.ds(pl.multiple_of(16 * b, 16), 16), j * LANES : (j + 1) * LANES] = both
        return carry

    lax.fori_loop(0, ROWS // 16, gather, 0)


def gated_rows(ids, picks, near, far, power, pole, res, skip, entry, product, query):
    return call(
        modal_kernel,
        jax.ShapeDtypeStruct((ROWS, CH), BF16),
        [SMEM_SPEC] * 2 + [VMEM_SPEC] * 9,
        [
            pltpu.VMEM((2, MODES) + WIDE, F32),
            pltpu.VMEM((2, MODES) + WIDE, F32),
            pltpu.VMEM((2, 8) + WIDE, F32),
            pltpu.VMEM((ROWS,) + WIDE, F32),
            pltpu.VMEM((ROWS // 8 * BLOCK, LANES), F32),
            pltpu.VMEM((BLOCK, LANES), F32),
        ],
        20,
        "gated_rows",
        12_000_000,
    )(ids, picks, near, far, power, pole, res, skip, entry, product, query)


def partial_products(blocks, places, weights, name):
    counts = [sum(part.stop - part.start for place in places for part, core in place if core == n) for n in range(2)]
    rows, total = counts[0], sum(counts)

    def kernel(*refs):
        block_refs, weight_refs = refs[: len(blocks)], refs[len(blocks) : -2]
        out_ref, all_rows = refs[-2:]
        y, x = lax.axis_index("y"), lax.axis_index("x")
        zl, core = lax.axis_index("zl"), lax.axis_index("core")
        at = [0, rows]
        for ref, place in zip(block_refs, places):
            for part, owner in place:
                count = part.stop - part.start
                all_rows[at[owner] : at[owner] + count] = ref[part, :]
                at[owner] += count
        for which in range(2):
            own_y, next_y, last_y = [ref[which] for ref in weight_refs[:3]]
            for shift, weight in enumerate((own_y, next_y, weight_refs[3 + which][...], last_y)):
                slot = (y + shift - x + 4) % 4
                to = pl.multiple_of((zl + which) % 2 * COLS, COLS)
                part = jnp.dot(all_rows[...], weight, preferred_element_type=F32).astype(BF16)
                if counts[1]:
                    out_ref[core, slot, :, pl.ds(to, COLS)] = part[:rows]
                    out_ref[1 - core, slot, :, pl.ds(to, COLS)] = part[rows:]
                else:
                    out_ref[0, slot, :, pl.ds(to, COLS)] = part

    return call(
        kernel,
        jax.ShapeDtypeStruct((2 if counts[1] else 1, 4, rows, 2 * COLS), BF16),
        [VMEM_SPEC] * (len(blocks) + 5),
        [pltpu.VMEM((total, CH), BF16)],
        24,
        name,
        1_000_000_000,
    )(*blocks, *weights)


def assemble_kernel(near_own, near_other, far, side, out_ref):
    zh, core = lax.axis_index("zh"), lax.axis_index("core")
    half = ROWS // 2
    same = pl.ds(pl.multiple_of(zh % 2 * 2 * COLS, 2 * COLS), 2 * COLS)
    other = pl.ds(pl.multiple_of((zh + 1) % 2 * 2 * COLS, 2 * COLS), 2 * COLS)

    @pl.when(zh // 2 == core)
    def _():
        out_ref[pl.ds(pl.multiple_of(core * half, half), half), same] = near_own[...]
        out_ref[pl.ds(pl.multiple_of((1 - core) * half, half), half), same] = near_other[...]

    @pl.when(zh // 2 != core)
    def _():
        out_ref[:, same] = far[...]

    out_ref[:, other] = side[...]


def add_complex(own, other, power):
    other = other.astype(F32)
    re = power[0] * other[0] - power[1] * other[1]
    im = power[0] * other[1] + power[1] * other[0]
    return own.astype(F32) + jnp.stack([re, im])


def shift_records(value, steps):
    return lax.ppermute(value, ("y", "zh", "zl"), [(i, i + steps) for i in range(32 - steps)])


def turn(value, axis, steps):
    return lax.ppermute(value, axis, [(i, (i + steps) % 4) for i in range(4)])


def tie(*values):
    return lax.optimization_barrier(values)


def shards(
    features, short_filter, decay, angle_rate, residues, skip, entry_states, segment_ids, state_ids, out_weight
):
    skip_row = skip.reshape(1, CH)
    border = shift_records(features[:, ROWS - 8 :, :], 1)
    pole, power, taps = prepare(segment_ids, short_filter.transpose(1, 0, 2), decay, angle_rate)
    power = power.reshape(4, 2, MODES * 8, LANES)
    border, out_weight, pole = tie(border, out_weight, pole)
    paired = lax.ppermute(out_weight, "zl", [(0, 1), (1, 0)])
    final, product = final_states(segment_ids, state_ids, features, border, taps, pole, entry_states)

    final, product = tie(final, product)
    last = [shift_records(final, steps) for steps in (3, 2, 1)][::-1]
    query = featured_query(segment_ids, features, border, taps)
    last, query, product, paired = tie(last, query, product, paired)
    leaving = final
    for n in range(3):
        leaving = add_complex(leaving, last[n], power[n])
    leaving = leaving.astype(BF16)
    entering = [shift_records(leaving, steps) for steps in (5, 1)][::-1]
    entering, out_weight, paired = tie(entering, out_weight, paired)
    here = jnp.stack([out_weight, paired])
    lower, upper = turn(here, "y", 1), turn(here, "y", -1)
    gated = gated_rows(
        segment_ids, state_ids, *entering, power, pole, residues, skip_row, entry_states, product, query
    )

    after, before = turn(gated, "zh", -1), turn(gated, "zh", 1)
    across, paired_across = turn(lower[0], "y", 1), turn(upper[1], "y", -1)
    weights = (here, upper, lower, across, paired_across)
    half = ROWS // 2
    top, bottom, whole = slice(0, half), slice(half, ROWS), slice(0, ROWS)
    after, before, weights = tie(after, before, weights)
    far = turn(after[top], "zh", -1), turn(before[bottom], "zh", 1)

    def over_cores(parts):
        other = lax.ppermute(parts[1], "core", [(0, 1), (1, 0)])
        return (parts[0].astype(F32) + other.astype(F32)).astype(BF16)

    def from_x(both, k):
        return turn(both[k], "x", k)

    def home(sums, moves):
        pairs = [(2 * zh + core, 2 * ((zh + step) % 4) + zh // 2) for zh in range(4) for core, step in moves]
        return lax.ppermute(sums, ("zh", "core"), pairs)

    def add(values):
        total = values[0].astype(F32)
        for value in values[1:]:
            total = total + value.astype(F32)
        return total.astype(BF16)

    places = [[(top, 0), (bottom, 1)], [(whole, 0)], [(whole, 1)]]
    one = over_cores(partial_products([gated, after, before], places, weights, "products_near"))
    one_x = [from_x(one, k) for k in (2, 1, 3)]
    far, one, one_x = tie(far, one, one_x)
    two = partial_products(far, [[(top, 0)], [(top, 0)]], weights, "products_far")[0]
    pairs = [(2 * zh + 1 - zh // 2, 2 * zh + zh // 2) for zh in range(4)]
    two = (two.astype(F32) + lax.ppermute(two, ("zh", "core"), pairs).astype(F32)).astype(BF16)
    one = add([one[0], *one_x])
    two_x = []
    for k in (2, 1, 3):
        pairs = [(8 * zh + 2 * x + zh // 2, 8 * zh + 2 * ((x + k) % 4) + zh // 2) for zh in range(4) for x in range(4)]
        two_x.append(lax.ppermute(two[k], ("zh", "x", "core"), pairs))
    two = add([two[0], *two_x])
    near_own = one[:half]
    near_other = lax.ppermute(near_own, "core", [(0, 1), (1, 0)])
    side = home(one[half:], [(0, 1), (1, 3)])
    pairs = [(2 * zh + zh // 2, 2 * ((zh + 2) % 4) + zh // 2) for zh in range(4)]
    far_sums = lax.ppermute(two, ("zh", "core"), pairs)
    return call(
        assemble_kernel, jax.ShapeDtypeStruct((ROWS, CH), BF16), [VMEM_SPEC] * 4, [], 8, "assemble", 1_000_000
    )(near_own, near_other, far_sums, side)


def solution(mesh):
    fine = Mesh(mesh.devices.reshape(4, 4, 2, 4, 2), ("y", "zh", "zl", "x", "core"))
    seq, chan = ("y", "zh", "zl"), ("x", "core")
    in_specs = (
        P(None, seq, chan),
        P(None, None, chan),
        P(None, chan),
        P(None, chan),
        P(None, None, chan),
        P(chan),
        P(None, None, None, chan),
        P(),
        P(),
        P(chan, seq),
    )
    return jax.shard_map(shards, mesh=fine, in_specs=in_specs, out_specs=P(seq, chan), check_vma=False)
```

```python
import jax
import jax.numpy as jnp
from jax import lax
from jax.experimental import pallas as pl
from jax.experimental.pallas import tpu as pltpu
from jax.sharding import Mesh
from jax.sharding import PartitionSpec as P

F32 = jnp.float32
BF16 = jnp.bfloat16
ROWS = 256
CH = 1024
LANES = 128
TILES = CH // LANES
MODES = 16
TAPS = 7
GROUP = 16
GAP = 9
BLOCK = GAP * TILES
COLS = 256
SPARE = 16
WIDE = (8, LANES)
MIB = 1024 * 1024
SMEM_SPEC = pl.BlockSpec(memory_space=pltpu.SMEM)
VMEM_SPEC = pl.BlockSpec(memory_space=pltpu.VMEM)


def call(kernel, outs, in_specs, scratch, limit, name, cycles, interpret=False):
    return pl.pallas_call(
        kernel,
        out_shape=outs,
        in_specs=in_specs,
        out_specs=jax.tree.map(lambda out: VMEM_SPEC, outs),
        scratch_shapes=scratch,
        compiler_params=pltpu.CompilerParams(vmem_limit_bytes=limit * MIB),
        cost_estimate=pl.CostEstimate(flops=cycles, transcendentals=0, bytes_accessed=MIB),
        name=name,
        interpret=interpret,
    )


def first_position():
    device = (lax.axis_index("y") * 4 + lax.axis_index("zh")) * 2 + lax.axis_index("zl")
    return device * ROWS


def spread(scratch, base, value):
    for j in range(TILES):
        scratch[pl.ds(base + j * GAP, value.shape[0]), :] = value[:, j * LANES : (j + 1) * LANES]


def row(scratch, base, r):
    return scratch[pl.ds(base + r, TILES, stride=GAP), :]


def record_of(ids, position):
    return jnp.where(position < 0, -1, ids[jnp.maximum(position, 0)])


def prepare_kernel(ids, filt, decay, angle, pole_out, power_out, taps_out, small):
    position = first_position()
    for half in range(2):
        rows = slice(8 * half, 8 * half + 8)
        mag = jnp.exp(-decay[rows, :])
        ang = angle[rows, :]
        spread(small, 0, mag * jnp.cos(ang))
        spread(small, BLOCK, mag * jnp.sin(ang))
        for r in range(8):
            pole_out[0, 0, 8 * half + r] = row(small, 0, r)
            pole_out[0, 1, 8 * half + r] = row(small, BLOCK, r)
    keeps = []
    for count, last in ((1, position + ROWS - 1), (2, position + ROWS - 1), (3, position + ROWS - 1), (4, position - 1)):
        before = last - count * ROWS
        keeps.append(jnp.where((before >= 0) & (record_of(ids, before) == record_of(ids, last)), 1.0, 0.0))
    for m in range(MODES):
        re, im = pole_out[0, 0, m], pole_out[0, 1, m]
        two_re, two_im = re * re - im * im, 2.0 * re * im
        pole_out[1, 0, m], pole_out[1, 1, m] = two_re, two_im
        pole_out[2, 0, m], pole_out[2, 1, m] = re * two_re - im * two_im, re * two_im + im * two_re
        re, im = two_re * two_re - two_im * two_im, 2.0 * two_re * two_im
        pole_out[3, 0, m], pole_out[3, 1, m] = re, im
        for doubling in range(6):
            re, im = re * re - im * im, 2.0 * re * im
        two_re, two_im = re * re - im * im, 2.0 * re * im
        powers = (
            (re, im),
            (two_re, two_im),
            (re * two_re - im * two_im, re * two_im + im * two_re),
            (two_re * two_re - two_im * two_im, 2.0 * two_re * two_im),
        )
        for n in range(4):
            power_out[n, 0, m] = powers[n][0] * keeps[n]
            power_out[n, 1, m] = powers[n][1] * keeps[n]
    groups = CH // GROUP
    group = lax.broadcasted_iota(jnp.int32, (groups, CH), 0)
    channel = lax.broadcasted_iota(jnp.int32, (groups, CH), 1)
    widen = jnp.where(channel // GROUP == group, 1.0, 0.0).astype(BF16)
    for i in range(3):
        spread(small, 0, jnp.dot(filt[i], widen, preferred_element_type=F32))
        for j in range(TAPS):
            taps_out[j, i] = row(small, 0, j)


def prepare(ids, filt, decay, angle):
    return call(
        prepare_kernel,
        (
            jax.ShapeDtypeStruct((4, 2, MODES) + WIDE, F32),
            jax.ShapeDtypeStruct((4, 2, MODES) + WIDE, F32),
            jax.ShapeDtypeStruct((TAPS, 3) + WIDE, F32),
        ),
        [SMEM_SPEC] + [VMEM_SPEC] * 3,
        [pltpu.VMEM((2 * BLOCK + SPARE, LANES), F32)],
        58,
        "prepare",
        3_000_000,
    )(ids, filt, decay, angle)


def lay_out(feat, which, streams):
    def step(b, carry):
        for n, i in enumerate(which):
            value = feat[i, pl.ds(pl.multiple_of(b * 16, 16), 16), :].astype(F32)
            spread(streams.at[n], 2 * b * BLOCK, value[:8])
            spread(streams.at[n], (2 * b + 1) * BLOCK, value[8:])
        return carry

    lax.fori_loop(0, ROWS // 16, step, 0)


def featurized(values, taps, same):
    outs = []
    for t in range(8):
        out = taps[0] * values[6 + t]
        for j in range(1, TAPS):
            value = values[6 + t - j]
            if same is not None:
                value = jnp.where(same[t][j], value, 0.0)
            out = out + taps[j] * value
        outs.append(out)
    return outs


def featurize(position, ids, which, streams, edge, taps, emit):
    def step(b, before):
        first = position + 8 * b
        plain = record_of(ids, first - 6) == ids[first + 7]
        rows = [[row(streams.at[n], b * BLOCK, r) for r in range(8)] for n in range(len(which))]

        def run(same):
            emit(
                b,
                [
                    featurized([*before[n], *rows[n]], [taps[j, i] for j in range(TAPS)], same)
                    for n, i in enumerate(which)
                ],
            )

        @pl.when(plain)
        def _():
            run(None)

        @pl.when(jnp.logical_not(plain))
        def _():
            run([[record_of(ids, first + t - j) == ids[first + t] for j in range(TAPS)] for t in range(8)])

        return tuple(tuple(eight[2:]) for eight in rows)

    lax.fori_loop(0, ROWS // 8, step, tuple(tuple(row(edge, i * BLOCK, 2 + r) for r in range(6)) for i in which))


def run_modes(position, ids, picks, entry, states, small, product, group, step, emit, carry_in=None, block_step=None):
    for part in range(2):
        for m in range(8):
            states[part, m] = jnp.zeros(WIDE, F32) if carry_in is None else carry_in[part, 8 * group + m]

    def block(b, carry):
        first = position + 8 * b
        plain = record_of(ids, first - 1) == ids[first + 7]

        @pl.when(plain)
        def _():
            re = [states[0, m] for m in range(8)]
            im = [states[1, m] for m in range(8)]
            if block_step is None:
                for t in range(8):
                    value = product[8 * b + t]
                    emit(8 * b + t, value, step(value, re, im))
            else:
                block_step([product[8 * b + t] for t in range(8)], re, im)
            for m in range(8):
                states[0, m] = re[m]
                states[1, m] = im[m]

        @pl.when(jnp.logical_not(plain))
        def _():
            def one(t, carry):
                here = first + t

                @pl.when(record_of(ids, here - 1) != ids[here])
                def _():
                    pick = picks[ids[here]]
                    for part in range(2):
                        spread(small, 0, entry[pick, part, 8 * group : 8 * group + 8, :])
                        for m in range(8):
                            states[part, m] = row(small, 0, m)

                re = [states[0, m] for m in range(8)]
                im = [states[1, m] for m in range(8)]
                value = product[8 * b + t]
                emit(8 * b + t, value, step(value, re, im))
                for m in range(8):
                    states[0, m] = re[m]
                    states[1, m] = im[m]
                return carry

            lax.fori_loop(0, 8, one, 0)

        return carry

    lax.fori_loop(0, ROWS // 8, block, 0)


def final_kernel(ids, picks, feat, border, taps, pole, entry, final_out, product_out, streams, edge, states, small):
    position = first_position()
    lay_out(feat, (1, 2), streams)
    for i in (1, 2):
        spread(edge, i * BLOCK, border[i].astype(F32))

    def emit(b, outs):
        for t in range(8):
            product_out[8 * b + t] = (outs[0][t] * outs[1][t]).astype(BF16).astype(F32)

    featurize(position, ids, (1, 2), streams, edge, taps, emit)
    for group in range(2):

        def step(value, re, im, group=group):
            for m in range(8):
                pr, pi = pole[0, 0, 8 * group + m], pole[0, 1, 8 * group + m]
                re[m], im[m] = pr * re[m] - pi * im[m] + value, pr * im[m] + pi * re[m]

        def block_step(values, re, im, group=group):
            for m in range(8):
                power_re = [pole[n, 0, 8 * group + m] for n in range(4)]
                power_im = [pole[n, 1, 8 * group + m] for n in range(4)]
                for at in (0, 4):
                    first, second, third, fourth = values[at : at + 4]
                    new_re = power_re[2] * first + power_re[1] * second + power_re[0] * third + fourth
                    new_im = power_im[2] * first + power_im[1] * second + power_im[0] * third
                    re[m], im[m] = (
                        power_re[3] * re[m] - power_im[3] * im[m] + new_re,
                        power_re[3] * im[m] + power_im[3] * re[m] + new_im,
                    )

        run_modes(
            position, ids, picks, entry, states, small, product_out, group, step, lambda at, value, out: None,
            block_step=block_step,
        )
        for part in range(2):
            for m in range(0, 8, 2):
                pair = jnp.concatenate([states[part, m], states[part, m + 1]], axis=0)
                at = 64 * group + 8 * m
                final_out[part, at : at + 16, :] = pair.astype(BF16)


def final_states(ids, picks, feat, border, taps, pole, entry):
    return call(
        final_kernel,
        (
            jax.ShapeDtypeStruct((2, MODES * 8, LANES), BF16),
            jax.ShapeDtypeStruct((ROWS,) + WIDE, F32),
        ),
        [SMEM_SPEC] * 2 + [VMEM_SPEC] * 5,
        [
            pltpu.VMEM((2, ROWS // 8 * BLOCK + SPARE, LANES), F32),
            pltpu.VMEM((3 * BLOCK + SPARE, LANES), F32),
            pltpu.VMEM((2, 8) + WIDE, F32),
            pltpu.VMEM((BLOCK + SPARE, LANES), F32),
        ],
        58,
        "final_states",
        8_000_000,
    )(ids, picks, feat, border, taps, pole, entry)


def query_kernel(ids, feat, border, taps, query_out, streams, edge):
    lay_out(feat, (0,), streams)
    spread(edge, 0, border[0].astype(F32))

    def emit(b, outs):
        for t in range(8):
            query_out[8 * b + t] = outs[0][t]

    featurize(first_position(), ids, (0,), streams, edge, taps, emit)


def featured_query(ids, feat, border, taps):
    return call(
        query_kernel,
        jax.ShapeDtypeStruct((ROWS,) + WIDE, F32),
        [SMEM_SPEC] + [VMEM_SPEC] * 3,
        [pltpu.VMEM((1, ROWS // 8 * BLOCK + SPARE, LANES), F32), pltpu.VMEM((BLOCK + SPARE, LANES), F32)],
        16,
        "featured_query",
        2_000_000,
    )(ids, feat, border, taps)


def residue_tables(res, tables, small, halves):
    for part in range(2):
        for half in halves:
            spread(small, 0, res[part, 8 * half : 8 * half + 8, :])
            for r in range(8):
                tables[part, 8 * half + r] = row(small, 0, r)


def modal_kernel(
    ids, picks, near, far, power, pole, res, skip, entry, product, query,
    gated_out, tables, carry_in, states, base, stage, small,
):
    for pair in range(MODES // 2):
        rows = slice(16 * pair, 16 * pair + 16)
        far_re, far_im = far[0, rows, :].astype(F32), far[1, rows, :].astype(F32)
        power_re, power_im = power[3, 0, rows, :], power[3, 1, rows, :]
        re = near[0, rows, :].astype(F32) + power_re * far_re - power_im * far_im
        im = near[1, rows, :].astype(F32) + power_re * far_im + power_im * far_re
        for part, value in enumerate((re, im)):
            carry_in[part, 2 * pair] = value[:8]
            carry_in[part, 2 * pair + 1] = value[8:]

    residue_tables(res, tables, small, (0, 1))
    spread(small, 0, skip[...])
    skip_row = row(small, 0, 0)
    for group in range(2):

        def step(value, re, im, group=group):
            out = None
            for m in range(8):
                mode = 8 * group + m
                pr, pi = pole[0, 0, mode], pole[0, 1, mode]
                new_re = pr * re[m] - pi * im[m] + value
                new_im = pr * im[m] + pi * re[m]
                re[m], im[m] = new_re, new_im
                term = tables[0, mode] * new_re - tables[1, mode] * new_im
                out = term if out is None else out + term
            return out

        def emit(at, value, out, group=group):
            if group == 0:
                base[at] = skip_row * value + out
            else:
                value = query[at] * (base[at] + out)
                stage[pl.ds(at // 8 * BLOCK + at % 8, TILES, stride=GAP), :] = value

        run_modes(first_position(), ids, picks, entry, states, small, product, group, step, emit, carry_in)

    def gather(b, carry):
        for j in range(TILES):
            low = stage[pl.ds(2 * b * BLOCK + j * GAP, 8), :]
            high = stage[pl.ds((2 * b + 1) * BLOCK + j * GAP, 8), :]
            both = jnp.concatenate([low, high], axis=0).astype(BF16)
            gated_out[pl.ds(pl.multiple_of(16 * b, 16), 16), j * LANES : (j + 1) * LANES] = both
        return carry

    lax.fori_loop(0, ROWS // 16, gather, 0)


def gated_rows(ids, picks, near, far, power, pole, res, skip, entry, product, query):
    return call(
        modal_kernel,
        jax.ShapeDtypeStruct((ROWS, CH), BF16),
        [SMEM_SPEC] * 2 + [VMEM_SPEC] * 9,
        [
            pltpu.VMEM((2, MODES) + WIDE, F32),
            pltpu.VMEM((2, MODES) + WIDE, F32),
            pltpu.VMEM((2, 8) + WIDE, F32),
            pltpu.VMEM((ROWS,) + WIDE, F32),
            pltpu.VMEM((ROWS // 8 * BLOCK + SPARE, LANES), F32),
            pltpu.VMEM((BLOCK + SPARE, LANES), F32),
        ],
        20,
        "gated_rows",
        12_000_000,
    )(ids, picks, near, far, power, pole, res, skip, entry, product, query)


def partial_products(blocks, places, weights, name):
    counts = [sum(part.stop - part.start for place in places for part, core in place if core == n) for n in range(2)]
    rows, total = counts[0], sum(counts)

    def kernel(*refs):
        block_refs, weight_refs = refs[: len(blocks)], refs[len(blocks) : -2]
        out_ref, all_rows = refs[-2:]
        y, x = lax.axis_index("y"), lax.axis_index("x")
        zl, core = lax.axis_index("zl"), lax.axis_index("core")
        at = [0, rows]
        for ref, place in zip(block_refs, places):
            for part, owner in place:
                count = part.stop - part.start
                all_rows[at[owner] : at[owner] + count] = ref[part, :]
                at[owner] += count
        for which in range(2):
            own_y, next_y, last_y = [ref[which] for ref in weight_refs[:3]]
            for shift, weight in enumerate((own_y, next_y, weight_refs[3 + which][...], last_y)):
                slot = (y + shift - x + 4) % 4
                to = pl.multiple_of((zl + which) % 2 * COLS, COLS)
                part = jnp.dot(all_rows[...], weight, preferred_element_type=F32).astype(BF16)
                if counts[1]:
                    out_ref[core, slot, :, pl.ds(to, COLS)] = part[:rows]
                    out_ref[1 - core, slot, :, pl.ds(to, COLS)] = part[rows:]
                else:
                    out_ref[0, slot, :, pl.ds(to, COLS)] = part

    return call(
        kernel,
        jax.ShapeDtypeStruct((2 if counts[1] else 1, 4, rows, 2 * COLS), BF16),
        [VMEM_SPEC] * (len(blocks) + 5),
        [pltpu.VMEM((total, CH), BF16)],
        24,
        name,
        1_000_000_000,
    )(*blocks, *weights)


def assemble_kernel(near_own, near_other, far, side, out_ref):
    zh, core = lax.axis_index("zh"), lax.axis_index("core")
    half = ROWS // 2
    same = pl.ds(pl.multiple_of(zh % 2 * 2 * COLS, 2 * COLS), 2 * COLS)
    other = pl.ds(pl.multiple_of((zh + 1) % 2 * 2 * COLS, 2 * COLS), 2 * COLS)

    @pl.when(zh // 2 == core)
    def _():
        out_ref[pl.ds(pl.multiple_of(core * half, half), half), same] = near_own[...]
        out_ref[pl.ds(pl.multiple_of((1 - core) * half, half), half), same] = near_other[...]

    @pl.when(zh // 2 != core)
    def _():
        out_ref[:, same] = far[...]

    out_ref[:, other] = side[...]


def add_complex(own, other, power):
    other = other.astype(F32)
    re = power[0] * other[0] - power[1] * other[1]
    im = power[0] * other[1] + power[1] * other[0]
    return own.astype(F32) + jnp.stack([re, im])


def shift_records(value, steps):
    return lax.ppermute(value, ("y", "zh", "zl"), [(i, i + steps) for i in range(32 - steps)])


def turn(value, axis, steps):
    return lax.ppermute(value, axis, [(i, (i + steps) % 4) for i in range(4)])


def tie(*values):
    return lax.optimization_barrier(values)


def shards(
    features, short_filter, decay, angle_rate, residues, skip, entry_states, segment_ids, state_ids, out_weight
):
    skip_row = skip.reshape(1, CH)
    border = shift_records(features[:, ROWS - 8 :, :], 1)
    pole, power, taps = prepare(segment_ids, short_filter.transpose(1, 0, 2), decay, angle_rate)
    power = power.reshape(4, 2, MODES * 8, LANES)
    border, out_weight, pole = tie(border, out_weight, pole)
    paired = lax.ppermute(out_weight, "zl", [(0, 1), (1, 0)])
    final, product = final_states(segment_ids, state_ids, features, border, taps, pole, entry_states)

    final, product = tie(final, product)
    last = [shift_records(final, steps) for steps in (3, 2, 1)][::-1]
    query = featured_query(segment_ids, features, border, taps)
    last, query, product, paired = tie(last, query, product, paired)
    leaving = final
    for n in range(3):
        leaving = add_complex(leaving, last[n], power[n])
    leaving = leaving.astype(BF16)
    entering = [shift_records(leaving, steps) for steps in (5, 1)][::-1]
    entering, out_weight, paired = tie(entering, out_weight, paired)
    here = jnp.stack([out_weight, paired])
    lower, upper = turn(here, "y", 1), turn(here, "y", -1)
    gated = gated_rows(
        segment_ids, state_ids, *entering, power, pole, residues, skip_row, entry_states, product, query
    )

    after, before = turn(gated, "zh", -1), turn(gated, "zh", 1)
    across, paired_across = turn(lower[0], "y", 1), turn(upper[1], "y", -1)
    weights = (here, upper, lower, across, paired_across)
    half = ROWS // 2
    top, bottom, whole = slice(0, half), slice(half, ROWS), slice(0, ROWS)
    after, before, weights = tie(after, before, weights)
    far = turn(after[top], "zh", -1), turn(before[bottom], "zh", 1)

    def over_cores(parts):
        other = lax.ppermute(parts[1], "core", [(0, 1), (1, 0)])
        return (parts[0].astype(F32) + other.astype(F32)).astype(BF16)

    def from_x(both, k):
        return turn(both[k], "x", k)

    def home(sums, moves):
        pairs = [(2 * zh + core, 2 * ((zh + step) % 4) + zh // 2) for zh in range(4) for core, step in moves]
        return lax.ppermute(sums, ("zh", "core"), pairs)

    def add(values):
        total = values[0].astype(F32)
        for value in values[1:]:
            total = total + value.astype(F32)
        return total.astype(BF16)

    places = [[(top, 0), (bottom, 1)], [(whole, 0)], [(whole, 1)]]
    one = over_cores(partial_products([gated, after, before], places, weights, "products_near"))
    one_x = [from_x(one, k) for k in (2, 1, 3)]
    far, one, one_x = tie(far, one, one_x)
    two = partial_products(far, [[(top, 0)], [(top, 0)]], weights, "products_far")[0]
    pairs = [(2 * zh + 1 - zh // 2, 2 * zh + zh // 2) for zh in range(4)]
    two = (two.astype(F32) + lax.ppermute(two, ("zh", "core"), pairs).astype(F32)).astype(BF16)
    one = add([one[0], *one_x])
    two_x = []
    for k in (2, 1, 3):
        pairs = [(8 * zh + 2 * x + zh // 2, 8 * zh + 2 * ((x + k) % 4) + zh // 2) for zh in range(4) for x in range(4)]
        two_x.append(lax.ppermute(two[k], ("zh", "x", "core"), pairs))
    two = add([two[0], *two_x])
    near_own = one[:half]
    near_other = lax.ppermute(near_own, "core", [(0, 1), (1, 0)])
    side = home(one[half:], [(0, 1), (1, 3)])
    pairs = [(2 * zh + zh // 2, 2 * ((zh + 2) % 4) + zh // 2) for zh in range(4)]
    far_sums = lax.ppermute(two, ("zh", "core"), pairs)
    return call(
        assemble_kernel, jax.ShapeDtypeStruct((ROWS, CH), BF16), [VMEM_SPEC] * 4, [], 8, "assemble", 1_000_000
    )(near_own, near_other, far_sums, side)


def solution(mesh):
    fine = Mesh(mesh.devices.reshape(4, 4, 2, 4, 2), ("y", "zh", "zl", "x", "core"))
    seq, chan = ("y", "zh", "zl"), ("x", "core")
    in_specs = (
        P(None, seq, chan),
        P(None, None, chan),
        P(None, chan),
        P(None, chan),
        P(None, None, chan),
        P(chan),
        P(None, None, None, chan),
        P(),
        P(),
        P(chan, seq),
    )
    return jax.shard_map(shards, mesh=fine, in_specs=in_specs, out_specs=P(seq, chan), check_vma=False)
```
